768 devices in a mesh: dp: 64 (over y, x, core), fsdp: 12 (over z).
Axes of the slice: x: 4, y: 8, z: 12, core: 2. Of those that a mesh axis runs over, the one named last changes fastest.
Arguments:
- enc_out: bfloat16 [12, 20480, 1408], P('fsdp', 'dp')
- norm_gain: float32 [1408], replicated, may hold values from 0.25 to 1.75
- norm_bias: float32 [1408], replicated, may hold values from -3 to 3
- w_e2d: bfloat16 [1408, 512], P('dp'), may hold values from -0.15625 to 0.15625
- token_index: int32 [12, 20480], P('fsdp', 'dp'), may hold values from 0 to 20479, as said below
- counts: int32 [12, 128], P('fsdp'), may hold values from 1 to 320, 20480 in all within a row
- owner: int32 [12, 128], P('fsdp'), may hold values from 0 to 127, each once within a row
- dec_tubes: int32 [12, 128, 512], P('fsdp', 'dp'), may hold values from 0 to 1567, as said below
- mask_token: float32 [512], replicated, may hold values from -4 to 4
- dec_gain: float32 [512], replicated, may hold values from 0.25 to 1.75
- dec_bias: float32 [512], replicated, may hold values from -3 to 3
- w_qkv: bfloat16 [512, 1536], P(None, 'fsdp')
- w_proj: bfloat16 [512, 512], replicated, may hold values from -0.25 to 0.25
- proj_bias: float32 [512], replicated, may hold values from -3 to 3
Outputs:
- dec_state: bfloat16 [12, 128, 512, 512], P('fsdp', 'dp')
The draws below stay inside these ranges and needn't reach their ends.
Inputs may be any that keep to these rules, and one draw needn't show every extreme that they name: `token_index`: in each group a permutation of all visible tokens; the 320 rows of one device hold, in rising order, the tokens of one residue modulo the devices of dp, so that one device holds at most 320 / (devices of dp) tokens of one clip. Each group's counts sum to 20480. `owner`: each group's slots are a permutation; slot s lies on the device of dp index s // 2. `dec_tubes`: each row holds 512 different tube numbers.
All inputs are finite; a program needn't handle non-finite values.
Results may differ from the reference program's by a relative error of at most 0.0089.
Values may be sent and summed in bfloat16 or wider, within the bound.
No kernel may reach another device: no remote copies, remote signals or barrier semaphores. Data moves between devices by JAX's collectives and lax.ppermute only.
A program may use at most 32 MiB of HBM per device.

```python
import math
import jax
import jax.numpy as jnp
import numpy as np
from jax import lax

D = 1408
DW = 512
DEC_HEADS = 8
TUBES = 1568
DEC_LEN = 512
VMAX = 320
TOK_DEV = 320
CLIPS_GRP = 128
GROUP_TOK = 20480
GROUPS = 12


def draw_enc_out(key, part):
    key_a, key_b, key_c = jax.random.split(key, 3)
    full_shape = (GROUPS, GROUP_TOK, D)
    col_scale = jnp.exp(jax.random.uniform(key_b, (D,), jnp.float32, math.log(0.3), math.log(3.0)))
    row_scale = jnp.exp(jax.random.uniform(key_c, (GROUPS, GROUP_TOK, 1), jnp.float32, math.log(0.3), math.log(3.0)))
    base_vals = jax.random.normal(key_a, full_shape, jnp.float32)
    values = base_vals * col_scale * row_scale
    return values.astype(jnp.bfloat16)


def draw_token_index(key, part):
    group_devices = GROUP_TOK // TOK_DEV
    group_keys = jax.random.split(key, GROUPS)
    residues = jax.vmap(lambda one_key: jax.random.permutation(one_key, group_devices))(group_keys)
    position = jnp.arange(GROUP_TOK, dtype=jnp.int32)
    device_of = position // TOK_DEV
    row_rank = position % TOK_DEV
    return (row_rank[None, :] * group_devices + residues[:, device_of]).astype(jnp.int32)


def draw_dec_tubes(key, part):
    row_keys = jax.random.split(key, GROUPS * CLIPS_GRP)
    chosen = jax.vmap(lambda one_key: jax.random.permutation(one_key, TUBES)[:DEC_LEN])(row_keys)
    return chosen.reshape(GROUPS, CLIPS_GRP, DEC_LEN).astype(jnp.int32)


def draw_w_qkv(key, part):
    key_a = jax.random.fold_in(key, 0)
    base_vals = jax.random.normal(key_a, (DW, 3 * DW), jnp.float32) * DW ** (-0.5)
    values = base_vals
    return values.astype(jnp.bfloat16)


def levels(stream_key, dims, cuts, smallest, top_value):
    gain, own = 1.0, jax.random.fold_in(stream_key, 6)
    for dim, shards_of in cuts:
        draws = jnp.exp(jax.random.uniform(jax.random.fold_in(own, dim), (shards_of,), jnp.float32, smallest / len(cuts), top_value / len(cuts)))
        gain = gain * jnp.repeat(draws, dims[dim] // shards_of).reshape([-1 if axis == dim else 1 for axis in range(len(dims))])
    return gain


def profile(count, total, bound, skew):
    loads = [(1 << 20) // math.isqrt(standing ** skew) + 1 for standing in range(2, count + 1)]
    spare, holding = total - bound - (count - 1), [1] * (count - 1)
    while spare > 0:
        movable = [i for i in range(count - 1) if holding[i] < bound]
        pool, left = sum([loads[i] for i in movable]), spare
        for i in movable:
            addition = min(bound - holding[i], max(1, left * loads[i] // pool), spare)
            holding[i] = holding[i] + addition
            spare = spare - addition
    return np.array([bound] + holding)


def uneven_parts(key, amount, total, bound, slope):
    if amount == 2:
        one = jax.random.randint(key, (), max(1, total - bound), min(bound, total - 1) + 1)
        return jnp.stack([one, total - one])
    lengths = jnp.asarray(profile(amount, total, bound, slope), jnp.int32)
    pairs = (amount - 1) // 2
    donor, sink = lengths[1:1 + 2 * pairs:2], lengths[2:2 + 2 * pairs:2]
    slack = jnp.minimum(donor - 1, bound - sink)
    moved = jax.random.randint(jax.random.fold_in(key, 1), (pairs,), 0, 1 << 20) % (slack + 1)
    lengths = lengths.at[1:1 + 2 * pairs:2].set(donor - moved).at[2:2 + 2 * pairs:2].set(sink + moved)
    return lengths[jax.random.permutation(jax.random.fold_in(key, 2), amount)]


def gaussian(stream_key, dims, deviation, bound, cuts=(), held_as=jnp.bfloat16):
    factor_of = levels(stream_key, dims, cuts, -0.22, 0.18) if cuts else 1.0
    values = jax.random.normal(stream_key, dims, jnp.float32) * deviation * factor_of
    return jnp.minimum(jnp.maximum(values, -bound), bound).astype(held_as)


def setup_inputs(seed: int = 0) -> dict:
    key_of = jax.random.split(jax.random.key(seed), 15)
    enc_out = draw_enc_out(jax.random.fold_in(key_of[14], 71), 0)
    norm_gain = jnp.clip(1.0 + 0.15 * jax.random.normal(key_of[1], (D,), jnp.float32), 0.25, 1.75)
    norm_bias = gaussian(key_of[2], (D,), 0.5, 3.0, (), jnp.float32)
    w_e2d = gaussian(key_of[3], (D, DW), D ** -0.5, 0.15625, ((0, 64),))
    token_index = draw_token_index(jax.random.fold_in(key_of[14], 71), 0)
    counts = jax.vmap(lambda own: uneven_parts(own, CLIPS_GRP, GROUP_TOK, VMAX, 2))(jax.random.split(key_of[5], GROUPS)).reshape((GROUPS, CLIPS_GRP)).astype(jnp.int32)
    owner = jax.vmap(lambda own: jax.random.permutation(own, CLIPS_GRP))(jax.random.split(key_of[6], GROUPS)).reshape((GROUPS, CLIPS_GRP)).astype(jnp.int32)
    dec_tubes = draw_dec_tubes(jax.random.fold_in(key_of[14], 71), 0)
    mask_token = gaussian(key_of[8], (DW,), 1.0, 4.0, (), jnp.float32)
    dec_gain = jnp.clip(1.0 + 0.15 * jax.random.normal(key_of[9], (DW,), jnp.float32), 0.25, 1.75)
    dec_bias = gaussian(key_of[10], (DW,), 0.5, 3.0, (), jnp.float32)
    w_qkv = draw_w_qkv(jax.random.fold_in(key_of[14], 71), 0)
    w_proj = gaussian(key_of[12], (DW, DW), DW ** -0.5, 0.25)
    proj_bias = gaussian(key_of[13], (DW,), 0.5, 3.0, (), jnp.float32)
    return dict(enc_out=enc_out, norm_gain=norm_gain, norm_bias=norm_bias, w_e2d=w_e2d, token_index=token_index, counts=counts, owner=owner, dec_tubes=dec_tubes, mask_token=mask_token, dec_gain=dec_gain, dec_bias=dec_bias, w_qkv=w_qkv, w_proj=w_proj, proj_bias=proj_bias)


def layer_norm(values, gain_vec, bias_vec):
    average = lax.optimization_barrier(jnp.mean(values, axis=-1, keepdims=True))
    centred = values - average
    spread = lax.optimization_barrier(jnp.mean(centred * centred, axis=-1, keepdims=True))
    return centred * lax.rsqrt(spread + 1e-06) * gain_vec + bias_vec

def tube_codes(tube_ids, code_width):
    column = jnp.arange(code_width, dtype=jnp.int32)
    exponent = (2 * (column // 2)).astype(jnp.float32) / code_width
    angles = tube_ids.astype(jnp.float32)[..., None] * jnp.power(jnp.float32(10000.0), -exponent)
    return jnp.where(column % 2 == 0, jnp.sin(angles), jnp.cos(angles))

def attend(queries, key_rows, value_rows, n_heads):
    length = queries.shape[0]
    head_width = queries.shape[1] // n_heads
    scale_factor = head_width ** (-0.5)

    def split_heads(matrix):
        return matrix.reshape(length, n_heads, head_width).transpose(1, 0, 2)

    def one_head(triple):
        query_h, key_h, value_h = triple
        scores = jnp.dot(query_h, key_h.T, preferred_element_type=jnp.float32) * scale_factor
        row_max = lax.optimization_barrier(jnp.max(scores, axis=-1, keepdims=True))
        expo_vals = jnp.exp(scores - row_max)
        weights = (expo_vals / lax.optimization_barrier(jnp.sum(expo_vals, axis=-1, keepdims=True))).astype(jnp.bfloat16)
        return jnp.dot(weights, value_h, preferred_element_type=jnp.float32).astype(jnp.bfloat16)
    outputs = lax.map(one_head, (split_heads(queries), split_heads(key_rows), split_heads(value_rows)))
    return outputs.transpose(1, 0, 2).reshape(length, n_heads * head_width)

def reference(enc_out, norm_gain, norm_bias, w_e2d, token_index, counts, owner, dec_tubes, mask_token, dec_gain, dec_bias, w_qkv, w_proj, proj_bias):
    dec_width = w_e2d.shape[1]

    def one_group(packed):
        features, held_ids, vis_counts, slot_ids, tubes = packed
        normed = layer_norm(features.astype(jnp.float32), norm_gain, norm_bias).astype(jnp.bfloat16)
        embedded = jnp.dot(normed, w_e2d, preferred_element_type=jnp.float32).astype(jnp.bfloat16)
        by_token = jnp.zeros_like(embedded).at[held_ids].set(embedded)
        first_ids = jnp.cumsum(vis_counts) - vis_counts
        clip_of_slot = jnp.zeros_like(slot_ids).at[slot_ids].set(jnp.arange(slot_ids.shape[0], dtype=jnp.int32))
        slot_first = first_ids[clip_of_slot]
        slot_count = vis_counts[clip_of_slot]
        slot_pos = jnp.arange(DEC_LEN, dtype=jnp.int32)
        source_ids = jnp.minimum(slot_first[:, None] + slot_pos[None, :], GROUP_TOK - 1)
        gathered = by_token[source_ids]
        visible = slot_pos[None, :] < slot_count[:, None]
        dec_input = jnp.where(visible[..., None], gathered.astype(jnp.float32), mask_token) + tube_codes(tubes, dec_width)
        dec_normed = layer_norm(dec_input, dec_gain, dec_bias).astype(jnp.bfloat16).reshape(-1, dec_width)
        projected = jnp.dot(dec_normed, w_qkv, preferred_element_type=jnp.float32).astype(jnp.bfloat16)
        projected = projected.reshape(CLIPS_GRP, DEC_LEN, 3 * dec_width)

        def per_slot(block):
            return attend(block[:, :dec_width], block[:, dec_width:2 * dec_width], block[:, 2 * dec_width:], DEC_HEADS)
        attended = lax.map(per_slot, projected)
        mixed = jnp.dot(attended.reshape(-1, dec_width), w_proj, preferred_element_type=jnp.float32)
        result = dec_input.reshape(-1, dec_width) + mixed + proj_bias
        return result.astype(jnp.bfloat16).reshape(CLIPS_GRP, DEC_LEN, dec_width)
    return lax.map(one_group, (enc_out, token_index, counts, owner, dec_tubes))
```

```python
import math

import jax
import jax.numpy as jnp
import numpy as np
from jax import lax
from jax.experimental import pallas as pl
from jax.experimental.pallas import tpu as pltpu
from jax.sharding import Mesh, PartitionSpec as P

DP = ("y", "x", "core")
PLANE = ("y", "x")
HEADS = 8
HEAD = 64
VMAX = 320
NDEV = 64
PER = 5
EPS = 1e-06
MIB = 1 << 20
BF = jnp.bfloat16
F32 = jnp.float32


def iota(shape, dim):
    return lax.broadcasted_iota(jnp.int32, shape, dim)


def prep_kernel(ids_ref, enc_ref, gain_ref, bias_ref, counts_ref, owner_ref, normed_ref, pick_ref, info_ref):
    residue = ids_ref[0]
    my_index = ids_ref[1]
    core = ids_ref[2]
    counts = counts_ref[...].astype(F32)
    row_id = iota((128, 128), 0)
    col_id = iota((128, 128), 1)
    counts_col = jnp.sum(jnp.where(row_id == col_id, counts, 0.0), axis=1, keepdims=True)
    first = jnp.sum(jnp.where(row_id < col_id, counts_col, 0.0), axis=0, keepdims=True)
    owner = owner_ref[...]
    start = jnp.floor((first + (63 - residue).astype(F32)) * (1.0 / 64.0))
    place = iota((640, 128), 0)
    dest = (place * 6554) >> 16
    rest = place - 10 * dest
    slot = 2 * dest + (rest & 1)
    target = jnp.sum(jnp.where(owner == slot, start, 0.0), axis=1, keepdims=True)
    target = target.astype(jnp.int32) + (rest >> 1)[:, :1]
    pick_ref[...] = jnp.where(iota((640, VMAX), 1) == target, 1.0, 0.0).astype(BF)
    line = iota((8, 128), 0)
    mine = 2 * my_index + (line & 1)
    held = jnp.where(line < 2, first, counts)
    info = jnp.sum(jnp.where(owner == mine, held, 0.0), axis=1, keepdims=True)
    info_ref[...] = jnp.broadcast_to(info, (8, 128)).astype(jnp.int32)
    values = enc_ref[...].astype(F32)
    average = jnp.mean(values, axis=1, keepdims=True)
    centred = values - average
    spread = jnp.mean(centred * centred, axis=1, keepdims=True)
    normed = (centred * lax.rsqrt(spread + EPS) * gain_ref[...] + bias_ref[...]).astype(BF)
    for half in range(2):
        side = core if half == 0 else 1 - core
        for tile, (low, high) in enumerate(((0, 512), (384, 1024), (896, 1408))):
            size = high - low
            column = iota((1, 256), 1) + 256 * tile
            block = (column * 2731) >> 16
            inner = column - 24 * block
            source = jnp.where(inner < 22, 44 * block + 22 * side + inner - low, -1)
            spread_out = jnp.where(iota((size, 256), 0) == source, 1.0, 0.0).astype(BF)
            normed_ref[half, :, 256 * tile : 256 * (tile + 1)] = jnp.dot(
                normed[:, low:high], spread_out, preferred_element_type=F32
            ).astype(BF)


def embed_kernel(normed_ref, own_ref, other_ref, pick_ref, out_ref, rows_ref):
    embedded = jnp.dot(normed_ref[0], own_ref[...], preferred_element_type=F32)
    embedded += jnp.dot(normed_ref[1], other_ref[...], preferred_element_type=F32)
    embedded = embedded.astype(BF)
    packed = jnp.dot(pick_ref[...], embedded, preferred_element_type=F32)
    for part in range(4):
        rows_ref[pl.ds(part, 640, stride=4), :] = packed[:, 128 * part : 128 * (part + 1)]
    out_ref[...] = rows_ref[...].astype(BF)


def decode_kernel(
    recv_ref, seat_ref, base_ref, gain_ref, bias_ref, wqk_ref, wvt_ref, wproj_ref, pbias_ref,
    out_ref, rows_ref, x_ref, vt_ref, att_ref,
):
    clip = pl.program_id(0)

    @pl.when(clip == 0)
    def _():
        rows_ref[...] = recv_ref[...].astype(F32)
        vt_ref[:, HEAD:, :] = jnp.ones((HEADS, 16, 512), BF)

    tokens = jnp.concatenate(
        [rows_ref[pl.ds(4 * clip + part, VMAX, stride=8), :] for part in range(4)], axis=1
    ).astype(BF)
    x_ref[:VMAX, :] = base_ref[:VMAX, :] + jnp.dot(seat_ref[0], tokens, preferred_element_type=F32)
    x_ref[VMAX:, :] = base_ref[VMAX:, :]
    values = x_ref[...]
    average = jnp.mean(values, axis=1, keepdims=True)
    centred = values - average
    spread = jnp.mean(centred * centred, axis=1, keepdims=True)
    normed = (centred * lax.rsqrt(spread + EPS) * gain_ref[...] + bias_ref[...]).astype(BF)
    across = (((1,), (1,)), ((), ()))
    queries = jnp.dot(normed, wqk_ref[:, :512], preferred_element_type=F32)
    queries = (queries * (HEAD**-0.5 * math.log2(math.e))).astype(BF)
    keys = jnp.dot(normed, wqk_ref[:, 512:], preferred_element_type=F32).astype(BF)
    vt = lax.dot_general(wvt_ref[...], normed, across, preferred_element_type=F32).astype(BF)
    for head in range(HEADS):
        vt_ref[head, :HEAD, :] = vt[HEAD * head : HEAD * (head + 1), :]
    left = iota((512, 128), 1) < HEAD
    zero = jnp.zeros((512, 128), BF)
    for head in range(HEADS):
        pair = slice(128 * (head // 2), 128 * (head // 2 + 1))
        key = keys[:, pair]
        key = jnp.where(left, key, zero) if head % 2 == 0 else jnp.where(left, zero, key)
        scores = lax.dot_general(key, queries[:, pair], across, preferred_element_type=F32)
        top = jnp.max(scores, axis=0, keepdims=True)
        weights = jnp.exp2(scores - top).astype(BF)
        mixed = jnp.dot(vt_ref[head], weights, preferred_element_type=F32)
        att_ref[HEAD * head : HEAD * (head + 1), :] = (
            mixed[:HEAD] * (1.0 / mixed[HEAD : HEAD + 1])
        ).astype(BF)
    result = lax.dot_general(
        att_ref[...], wproj_ref[...], (((0,), (0,)), ((), ())), preferred_element_type=F32
    )
    out_ref[0] = (x_ref[...] + result + pbias_ref[...]).astype(BF)


def whole(shape):
    return pl.BlockSpec(shape, lambda *_: (0,) * len(shape))


def on_device(
    enc_out, norm_gain, norm_bias, w_e2d, token_index, counts, owner, dec_tubes,
    mask_token, dec_gain, dec_bias, w_qkv, w_proj, proj_bias,
):
    my_index = lax.axis_index(DP).astype(jnp.int32)
    core = lax.axis_index("core").astype(jnp.int32)
    residue = token_index[0, 0] % NDEV
    w_full = lax.all_gather(w_qkv, "fsdp", axis=1, tiled=True)

    mark = jnp.broadcast_to(residue.astype(BF), (2, 512))
    shard = jnp.concatenate([w_e2d, mark], axis=0)
    gathered = lax.all_to_all(
        jnp.broadcast_to(shard[None], (32, 24, 512)), PLANE, 0, 0, tiled=True
    )
    own = gathered.reshape(768, 512)
    other = lax.ppermute(own, "core", [(0, 1), (1, 0)])

    ids = jnp.stack([residue, my_index, core])
    normed, pick, info = pl.pallas_call(
        prep_kernel,
        out_shape=(
            jax.ShapeDtypeStruct((2, VMAX, 768), BF),
            jax.ShapeDtypeStruct((640, VMAX), BF),
            jax.ShapeDtypeStruct((8, 128), jnp.int32),
        ),
        in_specs=[pl.BlockSpec(memory_space=pltpu.SMEM)] + [pl.BlockSpec(memory_space=pltpu.VMEM)] * 5,
        compiler_params=pltpu.CompilerParams(vmem_limit_bytes=24 * MIB),
        cost_estimate=pl.CostEstimate(flops=4_000_000_000, bytes_accessed=4_000_000, transcendentals=0),
        name="prep",
    )(ids, enc_out[0], norm_gain[None], norm_bias[None], counts, owner)

    sent = pl.pallas_call(
        embed_kernel,
        out_shape=jax.ShapeDtypeStruct((2560, 128), BF),
        scratch_shapes=[pltpu.VMEM((2560, 128), F32)],
        compiler_params=pltpu.CompilerParams(vmem_limit_bytes=24 * MIB),
        cost_estimate=pl.CostEstimate(flops=1_000_000_000, bytes_accessed=4_000_000, transcendentals=0),
        name="embed",
    )(normed, own, other, pick)
    received = lax.all_to_all(sent.reshape(NDEV, 40, 128), DP, 0, 0, tiled=True).reshape(2560, 128)

    column = np.arange(512)
    rate = np.power(10000.0, -(2 * (column // 2)) / 512.0).astype(np.float32)
    phase = np.where(column % 2 == 0, 0.0, math.pi / 2).astype(np.float32)
    codes = jnp.sin(dec_tubes[0].astype(F32)[..., None] * rate + phase)
    position = jnp.arange(512, dtype=jnp.int32)
    visible = position[None, :] < info[2:4, :1]
    base = jnp.where(visible[..., None], 0.0, mask_token) + codes

    own_mark = own.reshape(32, 24, 512)[:, 22, 0]
    other_mark = other.reshape(32, 24, 512)[:, 22, 0]
    first_mark = jnp.where(core == 0, own_mark, other_mark)
    second_mark = jnp.where(core == 0, other_mark, own_mark)
    marks = jnp.stack([first_mark, second_mark], axis=1).reshape(NDEV).astype(jnp.int32)
    offered = (marks[:, None] * 8 + jnp.arange(PER, dtype=jnp.int32)).reshape(NDEV * PER)
    rank = position[:VMAX]
    wanted = ((info[0:2, :1] + rank[None, :]) & 63) * 8 + (rank >> 6)[None, :]
    wanted = jnp.where(rank[None, :] < info[2:4, :1], wanted, -1)
    seat = (wanted[:, :, None] == offered[None, None, :]).astype(BF)

    return pl.pallas_call(
        decode_kernel,
        grid=(2,),
        out_shape=jax.ShapeDtypeStruct((1, 2, 512, 512), BF),
        in_specs=[
            whole((2560, 128)),
            pl.BlockSpec((1, VMAX, VMAX), lambda clip: (clip, 0, 0)),
            pl.BlockSpec((512, 512), lambda clip: (clip, 0)),
            whole((1, 512)),
            whole((1, 512)),
            whole((512, 1024)),
            whole((512, 512)),
            whole((512, 512)),
            whole((1, 512)),
        ],
        out_specs=pl.BlockSpec((None, 1, 512, 512), lambda clip: (0, clip, 0, 0)),
        scratch_shapes=[
            pltpu.VMEM((2560, 128), F32),
            pltpu.VMEM((512, 512), F32),
            pltpu.VMEM((HEADS, HEAD + 16, 512), BF),
            pltpu.VMEM((512, 512), BF),
        ],
        compiler_params=pltpu.CompilerParams(vmem_limit_bytes=32 * MIB),
        cost_estimate=pl.CostEstimate(flops=4_000_000_000, bytes_accessed=8_000_000, transcendentals=4_000_000),
        name="decode",
    )(
        received, seat, base.reshape(1024, 512), dec_gain[None], dec_bias[None],
        w_full[:, :1024], w_full[:, 1024:].T, w_proj, proj_bias[None],
    )


def solution(mesh):
    grid = Mesh(np.asarray(mesh.devices).reshape(8, 4, 2, 12), (*DP, "fsdp"))
    return jax.shard_map(
        on_device,
        mesh=grid,
        in_specs=(
            P("fsdp", DP, None), P(), P(), P(DP, None), P("fsdp", DP), P("fsdp", None), P("fsdp", None),
            P("fsdp", DP, None), P(), P(), P(), P(None, "fsdp"), P(), P(),
        ),
        out_specs=P("fsdp", DP, None, None),
        check_vma=False,
    )
```

```python
import math

import jax
import jax.numpy as jnp
import numpy as np
from jax import lax
from jax.experimental import pallas as pl
from jax.experimental.pallas import tpu as pltpu
from jax.sharding import Mesh, PartitionSpec as P

DP = ("y", "x", "core")
PLANE = ("y", "x")
HEADS = 8
HEAD = 64
VMAX = 320
NDEV = 64
PER = 5
EPS = 1e-06
MIB = 1 << 20
BF = jnp.bfloat16
F32 = jnp.float32


def iota(shape, dim):
    return lax.broadcasted_iota(jnp.int32, shape, dim)


def prep_kernel(ids_ref, enc_ref, gain_ref, bias_ref, counts_ref, owner_ref, normed_ref, pick_ref, info_ref):
    residue = ids_ref[0]
    my_index = ids_ref[1]
    core = ids_ref[2]
    counts = counts_ref[...].astype(F32)
    row_id = iota((128, 128), 0)
    col_id = iota((128, 128), 1)
    counts_col = jnp.sum(jnp.where(row_id == col_id, counts, 0.0), axis=1, keepdims=True)
    first = jnp.sum(jnp.where(row_id < col_id, counts_col, 0.0), axis=0, keepdims=True)
    owner = owner_ref[...]
    start = jnp.floor((first + (63 - residue).astype(F32)) * (1.0 / 64.0))
    place = iota((640, 128), 0)
    dest = (place * 6554) >> 16
    rest = place - 10 * dest
    slot = 2 * dest + (rest & 1)
    target = jnp.sum(jnp.where(owner == slot, start, 0.0), axis=1, keepdims=True)
    target = target.astype(jnp.int32) + (rest >> 1)[:, :1]
    pick_ref[...] = jnp.where(iota((640, VMAX), 1) == target, 1.0, 0.0).astype(BF)
    line = iota((8, 128), 0)
    mine = 2 * my_index + (line & 1)
    held = jnp.where(line < 2, first, counts)
    info = jnp.sum(jnp.where(owner == mine, held, 0.0), axis=1, keepdims=True)
    info_ref[...] = jnp.broadcast_to(info, (8, 128)).astype(jnp.int32)
    values = enc_ref[...].astype(F32)
    average = jnp.mean(values, axis=1, keepdims=True)
    centred = values - average
    spread = jnp.mean(centred * centred, axis=1, keepdims=True)
    normed = (centred * lax.rsqrt(spread + EPS) * gain_ref[...] + bias_ref[...]).astype(BF)
    for half in range(2):
        side = core if half == 0 else 1 - core
        for tile, (low, high) in enumerate(((0, 512), (384, 1024), (896, 1408))):
            size = high - low
            column = iota((1, 256), 1) + 256 * tile
            block = (column * 2731) >> 16
            inner = column - 24 * block
            source = jnp.where(inner < 22, 44 * block + 22 * side + inner - low, -1)
            spread_out = jnp.where(iota((size, 256), 0) == source, 1.0, 0.0).astype(BF)
            normed_ref[half, :, 256 * tile : 256 * (tile + 1)] = jnp.dot(
                normed[:, low:high], spread_out, preferred_element_type=F32
            ).astype(BF)


def embed_kernel(normed_ref, own_ref, other_ref, pick_ref, out_ref, rows_ref):
    embedded = jnp.dot(normed_ref[0], own_ref[...], preferred_element_type=F32)
    embedded += jnp.dot(normed_ref[1], other_ref[...], preferred_element_type=F32)
    embedded = embedded.astype(BF)
    packed = jnp.dot(pick_ref[...], embedded, preferred_element_type=F32)
    for part in range(4):
        rows_ref[pl.ds(part, 640, stride=4), :] = packed[:, 128 * part : 128 * (part + 1)]
    out_ref[...] = rows_ref[...].astype(BF)


def decode_kernel(
    recv_hbm, seat_hbm, base_hbm, wqk_hbm, wvt_hbm, wproj_hbm, gain_ref, bias_ref, pbias_ref,
    out_ref, recv_ref, seat_ref, base_ref, wqk_ref, wvt_ref, wproj_ref, rows_ref, x_ref, vt_ref, att_ref, sems,
):
    clip = pl.program_id(0)
    moves = [
        pltpu.make_async_copy(source, into, sems.at[n])
        for n, (source, into) in enumerate(
            (
                (recv_hbm, recv_ref), (seat_hbm, seat_ref), (base_hbm, base_ref),
                (wqk_hbm, wqk_ref), (wvt_hbm, wvt_ref), (wproj_hbm, wproj_ref),
            )
        )
    ]

    @pl.when(clip == 0)
    def _():
        for move in moves:
            move.start()
        vt_ref[:, HEAD:, :] = jnp.ones((HEADS, 16, 512), BF)
        moves[0].wait()
        rows_ref[...] = recv_ref[...].astype(F32)
        moves[1].wait()
        moves[2].wait()

    tokens = jnp.concatenate(
        [rows_ref[pl.ds(4 * clip + part, VMAX, stride=8), :] for part in range(4)], axis=1
    ).astype(BF)
    x_ref[:VMAX, :] = base_ref[clip, :VMAX, :] + jnp.dot(seat_ref[clip], tokens, preferred_element_type=F32)
    x_ref[VMAX:, :] = base_ref[clip, VMAX:, :]
    values = x_ref[...]
    average = jnp.mean(values, axis=1, keepdims=True)
    centred = values - average
    spread = jnp.mean(centred * centred, axis=1, keepdims=True)
    normed = (centred * lax.rsqrt(spread + EPS) * gain_ref[...] + bias_ref[...]).astype(BF)
    across = (((1,), (1,)), ((), ()))

    @pl.when(clip == 0)
    def _():
        for move in moves[3:]:
            move.wait()

    queries = jnp.dot(normed, wqk_ref[:, :512], preferred_element_type=F32)
    queries = (queries * (HEAD**-0.5 * math.log2(math.e))).astype(BF)
    keys = jnp.dot(normed, wqk_ref[:, 512:], preferred_element_type=F32).astype(BF)
    vt = lax.dot_general(wvt_ref[...], normed, across, preferred_element_type=F32).astype(BF)
    for head in range(HEADS):
        vt_ref[head, :HEAD, :] = vt[HEAD * head : HEAD * (head + 1), :]
    left = iota((512, 128), 1) < HEAD
    zero = jnp.zeros((512, 128), BF)
    for head in range(HEADS):
        pair = slice(128 * (head // 2), 128 * (head // 2 + 1))
        key = keys[:, pair]
        key = jnp.where(left, key, zero) if head % 2 == 0 else jnp.where(left, zero, key)
        scores = lax.dot_general(key, queries[:, pair], across, preferred_element_type=F32)
        top = jnp.max(scores, axis=0, keepdims=True)
        weights = jnp.exp2(scores - top).astype(BF)
        mixed = jnp.dot(vt_ref[head], weights, preferred_element_type=F32)
        att_ref[HEAD * head : HEAD * (head + 1), :] = (
            mixed[:HEAD] * (1.0 / mixed[HEAD : HEAD + 1])
        ).astype(BF)
    result = lax.dot_general(
        att_ref[...], wproj_ref[...], (((0,), (0,)), ((), ())), preferred_element_type=F32
    )
    out_ref[0] = (x_ref[...] + result + pbias_ref[...]).astype(BF)


def weights_kernel(where_ref, mine_ref, swap_ref, wqk_ref, wvt_ref):
    core = where_ref[12]
    for block in range(12):
        at = where_ref[block]
        for piece, side in ((mine_ref[at], core), (swap_ref[at], 1 - core)):
            rows = pl.ds(pl.multiple_of(256 * side, 256), 256)
            if block < 8:
                wqk_ref[rows, 128 * block : 128 * (block + 1)] = piece
            else:
                wvt_ref[128 * (block - 8) : 128 * (block - 7), rows] = piece.T


def gather_table():
    table = np.zeros((12, 12), np.int32)
    for z in range(12):
        for f in range(12):
            turn = (f // 4 - z // 4) % 3
            table[z, f] = 6 * ((f ^ z) & 1) + 3 * (((f ^ z) >> 1) & 1) + (0, 2, 1)[turn]
    return table


def gather_qkv(w_qkv, core):
    half = lax.dynamic_slice(w_qkv, (core * 256, 0), (256, 128))[None]
    above = lax.ppermute(half, "fsdp", [(z, (z + 4) % 12) for z in range(12)])
    below = lax.ppermute(half, "fsdp", [(z, (z + 8) % 12) for z in range(12)])
    three = jnp.concatenate([half, above, below])
    twin = lax.ppermute(three, "fsdp", [(z, z ^ 2) for z in range(12)])
    return three, twin


def place_qkv(three, twin, core):
    six = jnp.concatenate([three, twin])
    rest = lax.ppermute(six, "fsdp", [(z, z ^ 1) for z in range(12)])
    mine = jnp.concatenate([six, rest])
    swap = lax.ppermute(mine, "core", [(0, 1), (1, 0)])
    where = jnp.concatenate([jnp.asarray(gather_table())[lax.axis_index("fsdp")], core[None]])
    return pl.pallas_call(
        weights_kernel,
        out_shape=(pltpu.HBM((512, 1024), BF), pltpu.HBM((512, 512), BF)),
        in_specs=[pl.BlockSpec(memory_space=pltpu.SMEM)] + [pl.BlockSpec(memory_space=pltpu.VMEM)] * 2,
        compiler_params=pltpu.CompilerParams(vmem_limit_bytes=16 * MIB),
        cost_estimate=pl.CostEstimate(flops=0, bytes_accessed=6_000_000, transcendentals=0),
        name="weights",
    )(where, mine, swap)


def whole(shape):
    return pl.BlockSpec(shape, lambda *_: (0,) * len(shape))


def on_device(
    enc_out, norm_gain, norm_bias, w_e2d, token_index, counts, owner, dec_tubes,
    mask_token, dec_gain, dec_bias, w_qkv, w_proj, proj_bias,
):
    my_index = lax.axis_index(DP).astype(jnp.int32)
    core = lax.axis_index("core").astype(jnp.int32)
    residue = token_index[0, 0] % NDEV
    three, twin = gather_qkv(w_qkv, core)

    mark = jnp.broadcast_to(residue.astype(BF), (2, 512))
    shard = jnp.concatenate([w_e2d, mark], axis=0)
    shards = jnp.broadcast_to(shard[None], (32, 24, 512))
    gathered = lax.all_to_all(shards, PLANE, 0, 0, tiled=True)
    own = gathered.reshape(768, 512)
    other = lax.ppermute(own, "core", [(0, 1), (1, 0)])

    ids = jnp.stack([residue, my_index, core])
    normed, pick, info = pl.pallas_call(
        prep_kernel,
        out_shape=(
            jax.ShapeDtypeStruct((2, VMAX, 768), BF),
            jax.ShapeDtypeStruct((640, VMAX), BF),
            jax.ShapeDtypeStruct((8, 128), jnp.int32),
        ),
        in_specs=[pl.BlockSpec(memory_space=pltpu.SMEM)] + [pl.BlockSpec(memory_space=pltpu.VMEM)] * 5,
        compiler_params=pltpu.CompilerParams(vmem_limit_bytes=24 * MIB),
        cost_estimate=pl.CostEstimate(flops=4_000_000_000, bytes_accessed=4_000_000, transcendentals=0),
        name="prep",
    )(ids, enc_out[0], norm_gain[None], norm_bias[None], counts, owner)

    sent = pl.pallas_call(
        embed_kernel,
        out_shape=jax.ShapeDtypeStruct((2560, 128), BF),
        scratch_shapes=[pltpu.VMEM((2560, 128), F32)],
        compiler_params=pltpu.CompilerParams(vmem_limit_bytes=24 * MIB),
        cost_estimate=pl.CostEstimate(flops=1_000_000_000, bytes_accessed=4_000_000, transcendentals=0),
        name="embed",
    )(normed, own, other, pick)
    twin = lax.optimization_barrier((twin, sent))[0]
    wqk, wvt = place_qkv(three, twin, core)
    received = lax.all_to_all(sent.reshape(NDEV, 40, 128), DP, 0, 0, tiled=True)
    received = received.reshape(2560, 128)

    column = np.arange(512)
    rate = np.power(10000.0, -(2 * (column // 2)) / 512.0).astype(np.float32)
    phase = np.where(column % 2 == 0, 0.0, math.pi / 2).astype(np.float32)
    codes = jnp.sin(dec_tubes[0].astype(F32)[..., None] * rate + phase)
    position = jnp.arange(512, dtype=jnp.int32)
    visible = position[None, :] < info[2:4, :1]
    base = jnp.where(visible[..., None], 0.0, mask_token) + codes

    own_mark = own.reshape(32, 24, 512)[:, 22, 0]
    other_mark = other.reshape(32, 24, 512)[:, 22, 0]
    first_mark = jnp.where(core == 0, own_mark, other_mark)
    second_mark = jnp.where(core == 0, other_mark, own_mark)
    marks = jnp.stack([first_mark, second_mark], axis=1).reshape(NDEV).astype(jnp.int32)
    offered = (marks[:, None] * 8 + jnp.arange(PER, dtype=jnp.int32)).reshape(NDEV * PER)
    rank = position[:VMAX]
    wanted = ((info[0:2, :1] + rank[None, :]) & 63) * 8 + (rank >> 6)[None, :]
    wanted = jnp.where(rank[None, :] < info[2:4, :1], wanted, -1)
    seat = (wanted[:, :, None] == offered[None, None, :]).astype(BF)

    return pl.pallas_call(
        decode_kernel,
        grid=(2,),
        out_shape=jax.ShapeDtypeStruct((1, 2, 512, 512), BF),
        in_specs=[pl.BlockSpec(memory_space=pl.ANY)] + [pl.BlockSpec(memory_space=pltpu.HBM)] * 5 + [whole((1, 512))] * 3,
        out_specs=pl.BlockSpec((None, 1, 512, 512), lambda clip: (0, clip, 0, 0)),
        scratch_shapes=[
            pltpu.VMEM((2560, 128), BF),
            pltpu.VMEM((2, VMAX, VMAX), BF),
            pltpu.VMEM((2, 512, 512), F32),
            pltpu.VMEM((512, 1024), BF),
            pltpu.VMEM((512, 512), BF),
            pltpu.VMEM((512, 512), BF),
            pltpu.VMEM((2560, 128), F32),
            pltpu.VMEM((512, 512), F32),
            pltpu.VMEM((HEADS, HEAD + 16, 512), BF),
            pltpu.VMEM((512, 512), BF),
            pltpu.SemaphoreType.DMA((6,)),
        ],
        compiler_params=pltpu.CompilerParams(vmem_limit_bytes=53 * MIB),
        cost_estimate=pl.CostEstimate(flops=4_000_000_000, bytes_accessed=8_000_000, transcendentals=4_000_000),
        name="decode",
    )(
        received, seat, base, wqk, wvt, w_proj, dec_gain[None], dec_bias[None], proj_bias[None],
    )


def solution(mesh):
    grid = Mesh(np.asarray(mesh.devices).reshape(8, 4, 2, 12), (*DP, "fsdp"))
    return jax.shard_map(
        on_device,
        mesh=grid,
        in_specs=(
            P("fsdp", DP, None), P(), P(), P(DP, None), P("fsdp", DP), P("fsdp", None), P("fsdp", None),
            P("fsdp", DP, None), P(), P(), P(), P(None, "fsdp"), P(), P(),
        ),
        out_specs=P("fsdp", DP, None, None),
        check_vma=False,
    )
```

```python
import math

import jax
import jax.numpy as jnp
import numpy as np
from jax import lax
from jax.experimental import pallas as pl
from jax.experimental.pallas import tpu as pltpu
from jax.sharding import Mesh, PartitionSpec as P

DP = ("y", "x", "core")
PLANE = ("y", "x")
HEAD = 64
VMAX = 320
NDEV = 64
PER = 5
FIRST = 53
SECOND = 53
EPS = 1e-06
MIB = 1 << 20
BF = jnp.bfloat16
F32 = jnp.float32


def iota(shape, dim):
    return lax.broadcasted_iota(jnp.int32, shape, dim)


def prep_kernel(ids_ref, enc_ref, gain_ref, bias_ref, counts_ref, owner_ref, normed_ref, pick_ref, info_ref):
    residue = ids_ref[0]
    my_index = ids_ref[1]
    core = ids_ref[2]
    counts = counts_ref[...].astype(F32)
    row_id = iota((128, 128), 0)
    col_id = iota((128, 128), 1)
    counts_col = jnp.sum(jnp.where(row_id == col_id, counts, 0.0), axis=1, keepdims=True)
    first = jnp.sum(jnp.where(row_id < col_id, counts_col, 0.0), axis=0, keepdims=True)
    owner = owner_ref[...]
    start = jnp.floor((first + (63 - residue).astype(F32)) * (1.0 / 64.0))
    place = iota((640, 128), 0)
    dest = (place * 6554) >> 16
    rest = place - 10 * dest
    slot = 2 * dest + (rest & 1)
    target = jnp.sum(jnp.where(owner == slot, start, 0.0), axis=1, keepdims=True)
    target = target.astype(jnp.int32) + (rest >> 1)[:, :1]
    pick_ref[...] = jnp.where(iota((640, VMAX), 1) == target, 1.0, 0.0).astype(BF)
    line = iota((8, 128), 0)
    mine = 2 * my_index + (line & 1)
    held = jnp.where(line < 2, first, counts)
    info = jnp.sum(jnp.where(owner == mine, held, 0.0), axis=1, keepdims=True)
    info_ref[...] = jnp.broadcast_to(info, (8, 128)).astype(jnp.int32)
    values = enc_ref[...].astype(F32)
    average = jnp.mean(values, axis=1, keepdims=True)
    centred = values - average
    spread = jnp.mean(centred * centred, axis=1, keepdims=True)
    normed = (centred * lax.rsqrt(spread + EPS) * gain_ref[...] + bias_ref[...]).astype(BF)
    for half in range(2):
        side = core if half == 0 else 1 - core
        for tile, (low, high) in enumerate(((0, 512), (384, 1024), (896, 1408))):
            size = high - low
            column = iota((1, 256), 1) + 256 * tile
            block = (column * 2731) >> 16
            inner = column - 24 * block
            source = jnp.where(inner < 22, 44 * block + 22 * side + inner - low, -1)
            spread_out = jnp.where(iota((size, 256), 0) == source, 1.0, 0.0).astype(BF)
            normed_ref[half, :, 256 * tile : 256 * (tile + 1)] = jnp.dot(
                normed[:, low:high], spread_out, preferred_element_type=F32
            ).astype(BF)


def embed_kernel(normed_ref, own_ref, other_ref, pick_ref, out_ref, rows_ref):
    embedded = jnp.dot(normed_ref[0], own_ref[...], preferred_element_type=F32)
    embedded += jnp.dot(normed_ref[1], other_ref[...], preferred_element_type=F32)
    embedded = embedded.astype(BF)
    packed = jnp.dot(pick_ref[...], embedded, preferred_element_type=F32)
    for part in range(4):
        rows_ref[pl.ds(part, 640, stride=4), :] = packed[:, 128 * part : 128 * (part + 1)]
    out_ref[...] = rows_ref[...].astype(BF)


def shard_kernel(ids_ref, rows_ref, out_ref):
    residue = (ids_ref[0, 0] & 63).astype(F32)
    mark = jnp.full((2, 512), residue, F32)
    block = jnp.concatenate([rows_ref[...].astype(F32), mark], axis=0).astype(BF)
    for chip in range(32):
        out_ref[chip] = block


def fetch_blocks(where_ref, mine_hbm, swap_hbm, weights_ref, sems):
    moves = []
    for pair in range(2):
        for kind in range(3):
            at = 3 * pair + where_ref[kind]
            column = 384 * pair + 128 * kind
            for source, side in ((mine_hbm, where_ref[3]), (swap_hbm, 1 - where_ref[3])):
                rows = pl.ds(pl.multiple_of(256 * side, 256), 256)
                moves.append(
                    pltpu.make_async_copy(
                        source.at[at], weights_ref.at[rows, column : column + 128], sems.at[len(moves)]
                    )
                )
    return moves


def two_pairs(normed, weights_ref, wproj_ref, where_ref, first, total):
    across = (((1,), (1,)), ((), ()))
    left = iota((512, 128), 1) < HEAD
    zero = jnp.zeros((512, 128), BF)
    ones = jnp.ones((16, 512), BF)
    for pair in range(2):
        made = jnp.dot(normed, weights_ref[:, 384 * pair : 384 * (pair + 1)], preferred_element_type=F32)
        queries = (made[:, :128] * (HEAD**-0.5 * math.log2(math.e))).astype(BF)
        keys = made[:, 128:256].astype(BF)
        values = made[:, 256:].T.astype(BF)
        parts = []
        for head in range(2):
            key = jnp.where(left, keys, zero) if head == 0 else jnp.where(left, zero, keys)
            scores = lax.dot_general(key, queries, across, preferred_element_type=F32)
            top = jnp.max(scores, axis=0, keepdims=True)
            weights = jnp.exp2(scores - top).astype(BF)
            stacked = jnp.concatenate([values[HEAD * head : HEAD * (head + 1)], ones], axis=0)
            mixed = jnp.dot(stacked, weights, preferred_element_type=F32)
            parts.append(mixed[:HEAD] * (1.0 / mixed[HEAD : HEAD + 1]))
        attended = jnp.concatenate(parts, axis=0).T.astype(BF)
        rows = pl.ds(pl.multiple_of(128 * where_ref[first + pair], 128), 128)
        total = total + jnp.dot(attended, wproj_ref[rows, :], preferred_element_type=F32)
    return total


def first_kernel(
    where_ref, recv_hbm, seat_hbm, base_hbm, mine_hbm, swap_hbm, wproj_hbm, gain_ref, bias_ref, pbias_ref,
    total_ref, normed_ref, recv_ref, seat_ref, base_ref, weights_ref, wproj_ref, rows_ref, sems,
):
    clip = pl.program_id(0)
    moves = [
        pltpu.make_async_copy(source, into, sems.at[12 + n])
        for n, (source, into) in enumerate(
            ((recv_hbm, recv_ref), (seat_hbm, seat_ref), (base_hbm, base_ref), (wproj_hbm, wproj_ref))
        )
    ]

    @pl.when(clip == 0)
    def _():
        for move in moves:
            move.start()
        for move in fetch_blocks(where_ref, mine_hbm, swap_hbm, weights_ref, sems):
            move.start()
        moves[0].wait()
        rows_ref[...] = recv_ref[...].astype(F32)
        moves[1].wait()
        moves[2].wait()

    tokens = jnp.concatenate(
        [rows_ref[pl.ds(4 * clip + part, VMAX, stride=8), :] for part in range(4)], axis=1
    ).astype(BF)
    placed = jnp.dot(seat_ref[clip], tokens, preferred_element_type=F32)
    values = jnp.concatenate([base_ref[clip, :VMAX, :] + placed, base_ref[clip, VMAX:, :]], axis=0)
    average = jnp.mean(values, axis=1, keepdims=True)
    centred = values - average
    spread = jnp.mean(centred * centred, axis=1, keepdims=True)
    normed = (centred * lax.rsqrt(spread + EPS) * gain_ref[...] + bias_ref[...]).astype(BF)
    normed_ref[0] = normed
    total_ref[0] = values + pbias_ref[...]

    @pl.when(clip == 0)
    def _():
        for move in fetch_blocks(where_ref, mine_hbm, swap_hbm, weights_ref, sems):
            move.wait()
        moves[3].wait()

    total_ref[0] = two_pairs(normed, weights_ref, wproj_ref, where_ref, 4, total_ref[0])


def second_kernel(
    where_ref, total_ref, normed_ref, mine_hbm, swap_hbm, wproj_ref, out_ref, weights_ref, sems
):
    @pl.when(pl.program_id(0) == 0)
    def _():
        moves = fetch_blocks(where_ref, mine_hbm, swap_hbm, weights_ref, sems)
        for move in moves:
            move.start()
        for move in moves:
            move.wait()

    out_ref[0] = two_pairs(normed_ref[0], weights_ref, wproj_ref, where_ref, 6, total_ref[0]).astype(BF)


def gather_table():
    table = np.zeros((12, 8), np.int32)
    for z in range(12):
        table[z, :3] = [(0, 2, 1)[(kind - z // 4) % 3] for kind in range(3)]
        table[z, 4:] = [z % 4, (z ^ 2) % 4, (z ^ 1) % 4, (z ^ 3) % 4]
    return table


def whole(shape):
    return pl.BlockSpec(shape, lambda *_: (0,) * len(shape))


def on_device(
    enc_out, norm_gain, norm_bias, w_e2d, token_index, counts, owner, dec_tubes,
    mask_token, dec_gain, dec_bias, w_qkv, w_proj, proj_bias,
):
    vmem = pl.BlockSpec(memory_space=pltpu.VMEM)
    smem = pl.BlockSpec(memory_space=pltpu.SMEM)
    hbm = pl.BlockSpec(memory_space=pltpu.HBM)
    my_index = lax.axis_index(DP).astype(jnp.int32)
    core = lax.axis_index("core").astype(jnp.int32)

    shards = pl.pallas_call(
        shard_kernel,
        out_shape=jax.ShapeDtypeStruct((32, 24, 512), BF),
        in_specs=[smem, vmem],
        compiler_params=pltpu.CompilerParams(vmem_limit_bytes=8 * MIB),
        name="shards",
    )(token_index, w_e2d)
    gathered = lax.all_to_all(shards, PLANE, 0, 0, tiled=True)
    own = gathered.reshape(768, 512)
    other = lax.ppermute(own, "core", [(0, 1), (1, 0)])

    half = lax.dynamic_slice(w_qkv, (core * 256, 0), (256, 128))[None]
    above = lax.ppermute(half, "fsdp", [(z, (z + 4) % 12) for z in range(12)])
    below = lax.ppermute(half, "fsdp", [(z, (z + 8) % 12) for z in range(12)])

    ids = jnp.stack([token_index[0, 0] & 63, my_index, core])
    normed, pick, info = pl.pallas_call(
        prep_kernel,
        out_shape=(
            jax.ShapeDtypeStruct((2, VMAX, 768), BF),
            jax.ShapeDtypeStruct((640, VMAX), BF),
            jax.ShapeDtypeStruct((8, 128), jnp.int32),
        ),
        in_specs=[smem] + [vmem] * 5,
        compiler_params=pltpu.CompilerParams(vmem_limit_bytes=24 * MIB),
        cost_estimate=pl.CostEstimate(flops=4_000_000_000, bytes_accessed=4_000_000, transcendentals=0),
        name="prep",
    )(ids, enc_out[0], norm_gain[None], norm_bias[None], counts, owner)

    sent = pl.pallas_call(
        embed_kernel,
        out_shape=jax.ShapeDtypeStruct((2560, 128), BF),
        scratch_shapes=[pltpu.VMEM((2560, 128), F32)],
        compiler_params=pltpu.CompilerParams(vmem_limit_bytes=24 * MIB),
        cost_estimate=pl.CostEstimate(flops=1_000_000_000, bytes_accessed=4_000_000, transcendentals=0),
        name="embed",
    )(normed, own, other, pick)

    above, below = lax.optimization_barrier((above, below, sent))[:2]
    three = jnp.concatenate([half, above, below])
    twin = lax.ppermute(three, "fsdp", [(z, z ^ 2) for z in range(12)])
    received = lax.all_to_all(sent.reshape(NDEV, 40, 128), DP, 0, 0, tiled=True)
    received = received.reshape(2560, 128)
    six = jnp.concatenate([three, twin])
    rest = lax.ppermute(six, "fsdp", [(z, z ^ 1) for z in range(12)])
    six_swap = lax.ppermute(six, "core", [(0, 1), (1, 0)])
    rest_swap = lax.ppermute(rest, "core", [(0, 1), (1, 0)])
    where = jnp.asarray(gather_table())[lax.axis_index("fsdp")]
    where = where + core * jnp.asarray(np.arange(8) == 3, np.int32)

    column = np.arange(512)
    rate = np.power(10000.0, -(2 * (column // 2)) / 512.0).astype(np.float32)
    phase = np.where(column % 2 == 0, 0.0, math.pi / 2).astype(np.float32)
    position = jnp.arange(512, dtype=jnp.int32)
    visible = position[None, :] < info[2:4, :1]
    codes = jnp.sin(dec_tubes[0].astype(F32)[..., None] * rate + phase)
    base = jnp.where(visible[..., None], 0.0, mask_token) + codes

    own_mark = own.reshape(32, 24, 512)[:, 22, 0]
    other_mark = other.reshape(32, 24, 512)[:, 22, 0]
    first_mark = jnp.where(core == 0, own_mark, other_mark)
    second_mark = jnp.where(core == 0, other_mark, own_mark)
    marks = jnp.stack([first_mark, second_mark], axis=1).reshape(NDEV).astype(jnp.int32)
    offered = (marks[:, None] * 8 + jnp.arange(PER, dtype=jnp.int32)).reshape(NDEV * PER)
    rank = position[:VMAX]
    wanted = ((info[0:2, :1] + rank[None, :]) & 63) * 8 + (rank >> 6)[None, :]
    wanted = jnp.where(rank[None, :] < info[2:4, :1], wanted, -1)
    seat = (wanted[:, :, None] == offered[None, None, :]).astype(BF)

    clip_block = pl.BlockSpec((1, 512, 512), lambda clip: (clip, 0, 0))
    total, dec_normed = pl.pallas_call(
        first_kernel,
        grid=(2,),
        out_shape=(jax.ShapeDtypeStruct((2, 512, 512), F32), jax.ShapeDtypeStruct((2, 512, 512), BF)),
        in_specs=[smem, pl.BlockSpec(memory_space=pl.ANY)] + [hbm] * 5 + [whole((1, 512))] * 3,
        out_specs=(clip_block, clip_block),
        scratch_shapes=[
            pltpu.VMEM((2560, 128), BF),
            pltpu.VMEM((2, VMAX, VMAX), BF),
            pltpu.VMEM((2, 512, 512), F32),
            pltpu.VMEM((512, 768), BF),
            pltpu.VMEM((512, 512), BF),
            pltpu.VMEM((2560, 128), F32),
            pltpu.SemaphoreType.DMA((16,)),
        ],
        compiler_params=pltpu.CompilerParams(vmem_limit_bytes=FIRST * MIB),
        cost_estimate=pl.CostEstimate(flops=2_000_000_000, bytes_accessed=8_000_000, transcendentals=2_000_000),
        name="heads1",
    )(where, received, seat, base, six, six_swap, w_proj, dec_gain[None], dec_bias[None], proj_bias[None])
    return pl.pallas_call(
        second_kernel,
        grid=(2,),
        out_shape=jax.ShapeDtypeStruct((1, 2, 512, 512), BF),
        in_specs=[smem, clip_block, clip_block, hbm, hbm, whole((512, 512))],
        out_specs=pl.BlockSpec((None, 1, 512, 512), lambda clip: (0, clip, 0, 0)),
        scratch_shapes=[pltpu.VMEM((512, 768), BF), pltpu.SemaphoreType.DMA((12,))],
        compiler_params=pltpu.CompilerParams(vmem_limit_bytes=SECOND * MIB),
        cost_estimate=pl.CostEstimate(flops=2_000_000_000, bytes_accessed=8_000_000, transcendentals=2_000_000),
        name="heads2",
    )(where, total, dec_normed, rest, rest_swap, w_proj)


def solution(mesh):
    grid = Mesh(np.asarray(mesh.devices).reshape(8, 4, 2, 12), (*DP, "fsdp"))
    return jax.shard_map(
        on_device,
        mesh=grid,
        in_specs=(
            P("fsdp", DP, None), P(), P(), P(DP, None), P("fsdp", DP), P("fsdp", None), P("fsdp", None),
            P("fsdp", DP, None), P(), P(), P(), P(None, "fsdp"), P(), P(),
        ),
        out_specs=P("fsdp", DP, None, None),
        check_vma=False,
    )
```

```python
import math

import jax
import jax.numpy as jnp
import numpy as np
from jax import lax
from jax.experimental import pallas as pl
from jax.experimental.pallas import tpu as pltpu
from jax.sharding import Mesh, PartitionSpec as P

DP = ("y", "x", "core")
PLANE = ("y", "x")
HEAD = 64
VMAX = 320
NDEV = 64
PER = 5
FIRST = 53
SECOND = 53
AHEAD = 2
CHUNK = 64
EPS = 1e-06
MIB = 1 << 20
BF = jnp.bfloat16
F32 = jnp.float32


def iota(shape, dim):
    return lax.broadcasted_iota(jnp.int32, shape, dim)


def prep_kernel(ids_ref, token_ref, enc_ref, gain_ref, bias_ref, counts_ref, owner_ref, normed_ref, pick_ref, info_ref):
    residue = token_ref[0, 0] & 63
    my_index = ids_ref[0]
    core = ids_ref[1]
    counts = counts_ref[...].astype(F32)
    row_id = iota((128, 128), 0)
    col_id = iota((128, 128), 1)
    counts_col = jnp.sum(jnp.where(row_id == col_id, counts, 0.0), axis=1, keepdims=True)
    first = jnp.sum(jnp.where(row_id < col_id, counts_col, 0.0), axis=0, keepdims=True)
    owner = owner_ref[...]
    start = jnp.floor((first + (63 - residue).astype(F32)) * (1.0 / 64.0))
    place = iota((640, 128), 0)
    dest = (place * 6554) >> 16
    rest = place - 10 * dest
    slot = 2 * dest + (rest & 1)
    target = jnp.sum(jnp.where(owner == slot, start, 0.0), axis=1, keepdims=True)
    target = target.astype(jnp.int32) + (rest >> 1)[:, :1]
    pick_ref[...] = jnp.where(iota((640, VMAX), 1) == target, 1.0, 0.0).astype(BF)
    line = iota((8, 128), 0)
    mine = 2 * my_index + (line & 1)
    held = jnp.where(line < 2, first, counts)
    info = jnp.sum(jnp.where(owner == mine, held, 0.0), axis=1, keepdims=True)
    info_ref[...] = jnp.broadcast_to(info, (8, 128)).astype(jnp.int32)
    values = enc_ref[...].astype(F32)
    average = jnp.mean(values, axis=1, keepdims=True)
    centred = values - average
    spread = jnp.mean(centred * centred, axis=1, keepdims=True)
    normed = (centred * lax.rsqrt(spread + EPS) * gain_ref[...] + bias_ref[...]).astype(BF)
    for half in range(2):
        side = core if half == 0 else 1 - core
        for tile, (low, high) in enumerate(((0, 512), (384, 1024), (896, 1408))):
            size = high - low
            column = iota((1, 256), 1) + 256 * tile
            block = (column * 2731) >> 16
            inner = column - 24 * block
            source = jnp.where(inner < 22, 44 * block + 22 * side + inner - low, -1)
            spread_out = jnp.where(iota((size, 256), 0) == source, 1.0, 0.0).astype(BF)
            normed_ref[half, :, 256 * tile : 256 * (tile + 1)] = jnp.dot(
                normed[:, low:high], spread_out, preferred_element_type=F32
            ).astype(BF)


def embed_kernel(normed_ref, own_ref, other_ref, pick_ref, out_ref, rows_ref):
    embedded = jnp.dot(normed_ref[0], own_ref[...], preferred_element_type=F32)
    embedded += jnp.dot(normed_ref[1], other_ref[...], preferred_element_type=F32)
    embedded = embedded.astype(BF)
    packed = jnp.dot(pick_ref[...], embedded, preferred_element_type=F32)
    for part in range(4):
        rows_ref[pl.ds(part, 640, stride=4), :] = packed[:, 128 * part : 128 * (part + 1)]
    out_ref[...] = rows_ref[...].astype(BF)


def shard_kernel(ids_ref, rows_ref, out_ref):
    residue = (ids_ref[0, 0] & 63).astype(F32)
    mark = jnp.full((2, 512), residue, F32)
    block = jnp.concatenate([rows_ref[...].astype(F32), mark], axis=0).astype(BF)
    for chip in range(32):
        out_ref[chip] = block


def fetch_blocks(where_ref, first, mine_hbm, swap_hbm, wproj_hbm, weights_ref, wproj_ref, sems):
    moves = []

    def move(source, into):
        moves.append(pltpu.make_async_copy(source, into, sems.at[len(moves)]))

    for pair in range(2):
        for kind in range(3):
            at = 3 * pair + where_ref[kind]
            column = 256 * kind + 128 * pair
            for source, side in ((mine_hbm, where_ref[3]), (swap_hbm, 1 - where_ref[3])):
                rows = pl.ds(pl.multiple_of(256 * side, 256), 256)
                move(source.at[at], weights_ref.at[rows, column : column + 128])
        rows = pl.ds(pl.multiple_of(128 * where_ref[first + pair], 128), 128)
        move(wproj_hbm.at[rows, :], wproj_ref.at[128 * pair : 128 * (pair + 1), :])
    return moves


def four_heads(normed, weights_ref, wproj_ref):
    across = (((1,), (1,)), ((), ()))
    left = iota((512, 128), 1) < HEAD
    zero = jnp.zeros((512, 128), BF)
    ones = jnp.ones((16, 512), BF)
    made = jnp.dot(normed, weights_ref[...], preferred_element_type=F32)
    queries = (made[:, :256] * (HEAD**-0.5 * math.log2(math.e))).astype(BF)
    keys = made[:, 256:512].astype(BF)
    values = made[:, 512:].T.astype(BF)

    def score(head):
        pair = slice(128 * (head // 2), 128 * (head // 2 + 1))
        key = keys[:, pair]
        key = jnp.where(left, key, zero) if head % 2 == 0 else jnp.where(left, zero, key)
        return lax.dot_general(key, queries[:, pair], across, preferred_element_type=F32)

    def mix(head, scores):
        top = jnp.max(scores, axis=0, keepdims=True)
        weights = jnp.exp2(scores - top).astype(BF)
        stacked = jnp.concatenate([values[HEAD * head : HEAD * (head + 1)], ones], axis=0)
        mixed = jnp.dot(stacked, weights, preferred_element_type=F32)
        return mixed[:HEAD] * (1.0 / mixed[HEAD : HEAD + 1])

    scored = [score(head) for head in range(AHEAD)]
    parts = []
    for head in range(4):
        if head + AHEAD < 4:
            scored.append(score(head + AHEAD))
        parts.append(mix(head, scored[head]))
    attended = jnp.concatenate(parts, axis=0).T.astype(BF)
    return jnp.dot(attended, wproj_ref[...], preferred_element_type=F32)


def first_kernel(
    where_ref, recv_hbm, seat_hbm, base_hbm, mine_hbm, swap_hbm, wproj_hbm, gain_ref, bias_ref, pbias_ref,
    total_ref, normed_ref, recv_ref, seat_ref, base_ref, weights_ref, wproj_ref, rows_ref, sems,
):
    clip = pl.program_id(0)
    moves = [
        pltpu.make_async_copy(source, into, sems.at[14 + n])
        for n, (source, into) in enumerate(
            ((recv_hbm, recv_ref), (seat_hbm, seat_ref), (base_hbm, base_ref))
        )
    ]
    blocks = fetch_blocks(where_ref, 4, mine_hbm, swap_hbm, wproj_hbm, weights_ref, wproj_ref, sems)

    @pl.when(clip == 0)
    def _():
        for move in moves + blocks:
            move.start()
        moves[0].wait()
        rows_ref[...] = recv_ref[...].astype(F32)
        moves[1].wait()
        moves[2].wait()

    tokens = jnp.concatenate(
        [rows_ref[pl.ds(4 * clip + part, VMAX, stride=8), :] for part in range(4)], axis=1
    ).astype(BF)
    total_ref[0, :VMAX, :] = jnp.dot(seat_ref[clip], tokens, preferred_element_type=F32)
    for low in range(0, 512, CHUNK):
        rows = slice(low, low + CHUNK)
        values = base_ref[clip, rows, :]
        if low < VMAX:
            values = values + total_ref[0, rows, :]
        average = jnp.mean(values, axis=1, keepdims=True)
        centred = values - average
        spread = jnp.mean(centred * centred, axis=1, keepdims=True)
        normed_ref[0, rows, :] = (
            centred * lax.rsqrt(spread + EPS) * gain_ref[...] + bias_ref[...]
        ).astype(BF)
        total_ref[0, rows, :] = values + pbias_ref[...]

    @pl.when(clip == 0)
    def _():
        for move in blocks:
            move.wait()

    total_ref[0] += four_heads(normed_ref[0], weights_ref, wproj_ref)


def second_kernel(
    where_ref, total_ref, normed_ref, mine_hbm, swap_hbm, wproj_hbm, out_ref, weights_ref, wproj_ref, sems
):
    @pl.when(pl.program_id(0) == 0)
    def _():
        moves = fetch_blocks(where_ref, 6, mine_hbm, swap_hbm, wproj_hbm, weights_ref, wproj_ref, sems)
        for move in moves:
            move.start()
        for move in moves:
            move.wait()

    share = four_heads(normed_ref[0], weights_ref, wproj_ref)
    out_ref[0] = (total_ref[0] + share).astype(BF)


def gather_table():
    table = np.zeros((12, 8), np.int32)
    for z in range(12):
        table[z, :3] = [(0, 2, 1)[(kind - z // 4) % 3] for kind in range(3)]
        table[z, 4:] = [z % 4, (z ^ 2) % 4, (z ^ 1) % 4, (z ^ 3) % 4]
    return table


def whole(shape):
    return pl.BlockSpec(shape, lambda *_: (0,) * len(shape))


def on_device(
    enc_out, norm_gain, norm_bias, w_e2d, token_index, counts, owner, dec_tubes,
    mask_token, dec_gain, dec_bias, w_qkv, w_proj, proj_bias,
):
    vmem = pl.BlockSpec(memory_space=pltpu.VMEM)
    smem = pl.BlockSpec(memory_space=pltpu.SMEM)
    hbm = pl.BlockSpec(memory_space=pltpu.HBM)
    my_index = lax.axis_index(DP).astype(jnp.int32)
    core = lax.axis_index("core").astype(jnp.int32)

    shards = pl.pallas_call(
        shard_kernel,
        out_shape=jax.ShapeDtypeStruct((32, 24, 512), BF),
        in_specs=[smem, vmem],
        compiler_params=pltpu.CompilerParams(vmem_limit_bytes=8 * MIB),
        name="shards",
    )(token_index, w_e2d)
    gathered = lax.all_to_all(shards, PLANE, 0, 0, tiled=True)
    own = gathered.reshape(768, 512)
    other = lax.ppermute(own, "core", [(0, 1), (1, 0)])

    half = lax.dynamic_slice(w_qkv, (core * 256, 0), (256, 128))[None]
    above = lax.ppermute(half, "fsdp", [(z, (z + 4) % 12) for z in range(12)])
    below = lax.ppermute(half, "fsdp", [(z, (z + 8) % 12) for z in range(12)])

    ids = jnp.stack([my_index, core])
    normed, pick, info = pl.pallas_call(
        prep_kernel,
        out_shape=(
            jax.ShapeDtypeStruct((2, VMAX, 768), BF),
            jax.ShapeDtypeStruct((640, VMAX), BF),
            jax.ShapeDtypeStruct((8, 128), jnp.int32),
        ),
        in_specs=[smem] * 2 + [vmem] * 5,
        compiler_params=pltpu.CompilerParams(vmem_limit_bytes=24 * MIB),
        cost_estimate=pl.CostEstimate(flops=4_000_000_000, bytes_accessed=4_000_000, transcendentals=0),
        name="prep",
    )(ids, token_index, enc_out[0], norm_gain[None], norm_bias[None], counts, owner)

    sent = pl.pallas_call(
        embed_kernel,
        out_shape=jax.ShapeDtypeStruct((2560, 128), BF),
        scratch_shapes=[pltpu.VMEM((2560, 128), F32)],
        compiler_params=pltpu.CompilerParams(vmem_limit_bytes=24 * MIB),
        cost_estimate=pl.CostEstimate(flops=1_000_000_000, bytes_accessed=4_000_000, transcendentals=0),
        name="embed",
    )(normed, own, other, pick)

    above, below = lax.optimization_barrier((above, below, sent))[:2]
    three = jnp.concatenate([half, above, below])
    twin = lax.ppermute(three, "fsdp", [(z, z ^ 2) for z in range(12)])
    received = lax.all_to_all(sent.reshape(NDEV, 40, 128), DP, 0, 0, tiled=True)
    received = received.reshape(2560, 128)
    six = jnp.concatenate([three, twin])
    rest = lax.ppermute(six, "fsdp", [(z, z ^ 1) for z in range(12)])
    six_swap = lax.ppermute(six, "core", [(0, 1), (1, 0)])
    rest_swap = lax.ppermute(rest, "core", [(0, 1), (1, 0)])
    where = jnp.asarray(gather_table())[lax.axis_index("fsdp")]
    where = where + core * jnp.asarray(np.arange(8) == 3, np.int32)

    column = np.arange(512)
    rate = np.power(10000.0, -(2 * (column // 2)) / 512.0).astype(np.float32)
    phase = np.where(column % 2 == 0, 0.0, math.pi / 2).astype(np.float32)
    position = jnp.arange(512, dtype=jnp.int32)
    visible = position[None, :] < info[2:4, :1]
    codes = jnp.sin(dec_tubes[0].astype(F32)[..., None] * rate + phase)
    base = jnp.where(visible[..., None], 0.0, mask_token) + codes

    own_mark = own.reshape(32, 24, 512)[:, 22, 0]
    other_mark = other.reshape(32, 24, 512)[:, 22, 0]
    first_mark = jnp.where(core == 0, own_mark, other_mark)
    second_mark = jnp.where(core == 0, other_mark, own_mark)
    marks = jnp.stack([first_mark, second_mark], axis=1).reshape(NDEV).astype(jnp.int32)
    offered = (marks[:, None] * 8 + jnp.arange(PER, dtype=jnp.int32)).reshape(NDEV * PER)
    rank = position[:VMAX]
    wanted = ((info[0:2, :1] + rank[None, :]) & 63) * 8 + (rank >> 6)[None, :]
    wanted = jnp.where(rank[None, :] < info[2:4, :1], wanted, -1)
    seat = (wanted[:, :, None] == offered[None, None, :]).astype(BF)

    clip_block = pl.BlockSpec((1, 512, 512), lambda clip: (clip, 0, 0))
    total, dec_normed = pl.pallas_call(
        first_kernel,
        grid=(2,),
        out_shape=(jax.ShapeDtypeStruct((2, 512, 512), F32), jax.ShapeDtypeStruct((2, 512, 512), BF)),
        in_specs=[smem, pl.BlockSpec(memory_space=pl.ANY)] + [hbm] * 5 + [whole((1, 512))] * 3,
        out_specs=(clip_block, clip_block),
        scratch_shapes=[
            pltpu.VMEM((2560, 128), BF),
            pltpu.VMEM((2, VMAX, VMAX), BF),
            pltpu.VMEM((2, 512, 512), F32),
            pltpu.VMEM((512, 768), BF),
            pltpu.VMEM((256, 512), BF),
            pltpu.VMEM((2560, 128), F32),
            pltpu.SemaphoreType.DMA((17,)),
        ],
        compiler_params=pltpu.CompilerParams(vmem_limit_bytes=FIRST * MIB),
        cost_estimate=pl.CostEstimate(flops=2_000_000_000, bytes_accessed=8_000_000, transcendentals=2_000_000),
        name="heads1",
    )(where, received, seat, base, six, six_swap, w_proj, dec_gain[None], dec_bias[None], proj_bias[None])
    return pl.pallas_call(
        second_kernel,
        grid=(2,),
        out_shape=jax.ShapeDtypeStruct((1, 2, 512, 512), BF),
        in_specs=[smem, clip_block, clip_block, hbm, hbm, hbm],
        out_specs=pl.BlockSpec((None, 1, 512, 512), lambda clip: (0, clip, 0, 0)),
        scratch_shapes=[
            pltpu.VMEM((512, 768), BF),
            pltpu.VMEM((256, 512), BF),
            pltpu.SemaphoreType.DMA((14,)),
        ],
        compiler_params=pltpu.CompilerParams(vmem_limit_bytes=SECOND * MIB),
        cost_estimate=pl.CostEstimate(flops=2_000_000_000, bytes_accessed=8_000_000, transcendentals=2_000_000),
        name="heads2",
    )(where, total, dec_normed, rest, rest_swap, w_proj)


def solution(mesh):
    grid = Mesh(np.asarray(mesh.devices).reshape(8, 4, 2, 12), (*DP, "fsdp"))
    return jax.shard_map(
        on_device,
        mesh=grid,
        in_specs=(
            P("fsdp", DP, None), P(), P(), P(DP, None), P("fsdp", DP), P("fsdp", None), P("fsdp", None),
            P("fsdp", DP, None), P(), P(), P(), P(None, "fsdp"), P(), P(),
        ),
        out_specs=P("fsdp", DP, None, None),
        check_vma=False,
    )
```

```python
import math

import jax
import jax.numpy as jnp
import numpy as np
from jax import lax
from jax.experimental import pallas as pl
from jax.experimental.pallas import tpu as pltpu
from jax.sharding import Mesh, PartitionSpec as P

DP = ("y", "x", "core")
PLANE = ("y", "x")
HEAD = 64
VMAX = 320
NDEV = 64
PER = 5
FIRST = 53
CODES = 16
SECOND = 53
AHEAD = 2
CHUNK = 64
EPS = 1e-06
MIB = 1 << 20
BF = jnp.bfloat16
F32 = jnp.float32


def iota(shape, dim):
    return lax.broadcasted_iota(jnp.int32, shape, dim)


def prep_kernel(ids_ref, token_ref, enc_ref, gain_ref, bias_ref, counts_ref, owner_ref, normed_ref, pick_ref, info_ref):
    residue = token_ref[0, 0] & 63
    my_index = ids_ref[0]
    core = ids_ref[1]
    counts = counts_ref[...].astype(F32)
    row_id = iota((128, 128), 0)
    col_id = iota((128, 128), 1)
    counts_col = jnp.sum(jnp.where(row_id == col_id, counts, 0.0), axis=1, keepdims=True)
    first = jnp.sum(jnp.where(row_id < col_id, counts_col, 0.0), axis=0, keepdims=True)
    owner = owner_ref[...]
    start = jnp.floor((first + (63 - residue).astype(F32)) * (1.0 / 64.0))
    place = iota((640, 128), 0)
    dest = (place * 6554) >> 16
    rest = place - 10 * dest
    slot = 2 * dest + (rest & 1)
    target = jnp.sum(jnp.where(owner == slot, start, 0.0), axis=1, keepdims=True)
    target = target.astype(jnp.int32) + (rest >> 1)[:, :1]
    pick_ref[...] = jnp.where(iota((640, VMAX), 1) == target, 1.0, 0.0).astype(BF)
    line = iota((8, 128), 0)
    mine = 2 * my_index + (line & 1)
    held = jnp.where(line < 2, first, counts)
    info = jnp.sum(jnp.where(owner == mine, held, 0.0), axis=1, keepdims=True)
    info_ref[...] = jnp.broadcast_to(info, (8, 128)).astype(jnp.int32)
    values = enc_ref[...].astype(F32)
    average = jnp.mean(values, axis=1, keepdims=True)
    centred = values - average
    spread = jnp.mean(centred * centred, axis=1, keepdims=True)
    normed = (centred * lax.rsqrt(spread + EPS) * gain_ref[...] + bias_ref[...]).astype(BF)
    for half in range(2):
        side = core if half == 0 else 1 - core
        for tile, (low, high) in enumerate(((0, 512), (384, 1024), (896, 1408))):
            size = high - low
            column = iota((1, 256), 1) + 256 * tile
            block = (column * 2731) >> 16
            inner = column - 24 * block
            source = jnp.where(inner < 22, 44 * block + 22 * side + inner - low, -1)
            spread_out = jnp.where(iota((size, 256), 0) == source, 1.0, 0.0).astype(BF)
            normed_ref[half, :, 256 * tile : 256 * (tile + 1)] = jnp.dot(
                normed[:, low:high], spread_out, preferred_element_type=F32
            ).astype(BF)


def embed_kernel(normed_ref, own_ref, other_ref, pick_ref, out_ref, rows_ref):
    embedded = jnp.dot(normed_ref[0], own_ref[...], preferred_element_type=F32)
    embedded += jnp.dot(normed_ref[1], other_ref[...], preferred_element_type=F32)
    embedded = embedded.astype(BF)
    packed = jnp.dot(pick_ref[...], embedded, preferred_element_type=F32)
    for part in range(4):
        rows_ref[pl.ds(part, 640, stride=4), :] = packed[:, 128 * part : 128 * (part + 1)]
    out_ref[...] = rows_ref[...].astype(BF)


def shard_kernel(ids_ref, rows_ref, out_ref):
    residue = (ids_ref[0, 0] & 63).astype(F32)
    mark = jnp.full((2, 512), residue, F32)
    block = jnp.concatenate([rows_ref[...].astype(F32), mark], axis=0).astype(BF)
    for chip in range(32):
        out_ref[chip] = block


def turn_table():
    column = np.arange(512)
    turns = np.power(10000.0, -(2 * (column // 2)) / 512.0) / (2 * math.pi)
    scale = np.exp2(np.floor(np.log2(turns)) - 10)
    high = np.floor(turns / scale) * scale
    return np.stack([high, turns - high, 0.25 * (column % 2)]).astype(np.float32)


def codes_kernel(tubes_ref, table_ref, mask_ref, info_ref, offered_ref, base_ref, seat_ref):
    info = info_ref[...]
    for clip in range(2):
        tubes = jnp.broadcast_to(tubes_ref[clip : clip + 1, :].astype(F32), (8, 512)).T[:, :1]
        count = info[2 + clip : 3 + clip, :1]
        for low in range(0, 512, 64):
            tube = tubes[low : low + 64]
            whole_turns = tube * table_ref[0:1, :]
            turn = whole_turns - jnp.round(whole_turns) + (tube * table_ref[1:2, :] + table_ref[2:3, :])
            turn = turn - jnp.round(turn)
            size = jnp.abs(turn)
            angle = jnp.minimum(size, 0.5 - size) * (2 * math.pi)
            square = angle * angle
            series = 1.0 / 362880 - square * (1.0 / 39916800)
            for power in (5040, 120, 6, 1):
                series = 1.0 / power - square * series
            sine = angle * series
            code = jnp.where(turn < 0, -sine, sine)
            hidden = iota((64, 512), 0) + low >= count
            base_ref[clip, low : low + 64, :] = jnp.where(hidden, mask_ref[...], 0.0) + code
        rank = iota((VMAX, 1), 0)
        wanted = ((info[clip : clip + 1, :1] + rank) & 63) * 8 + (rank >> 6)
        wanted = jnp.where(rank < count, wanted, -1)
        seat_ref[clip] = jnp.where(offered_ref[...] == wanted, 1.0, 0.0).astype(BF)


def fetch_blocks(where_ref, first, mine_hbm, swap_hbm, wproj_hbm, weights_ref, wproj_ref, sems):
    moves = []

    def move(source, into):
        moves.append(pltpu.make_async_copy(source, into, sems.at[len(moves)]))

    for pair in range(2):
        for kind in range(3):
            at = 3 * pair + where_ref[kind]
            column = 256 * kind + 128 * pair
            for source, side in ((mine_hbm, where_ref[3]), (swap_hbm, 1 - where_ref[3])):
                rows = pl.ds(pl.multiple_of(256 * side, 256), 256)
                move(source.at[at], weights_ref.at[rows, column : column + 128])
        rows = pl.ds(pl.multiple_of(128 * where_ref[first + pair], 128), 128)
        move(wproj_hbm.at[rows, :], wproj_ref.at[128 * pair : 128 * (pair + 1), :])
    return moves


def four_heads(normed, weights_ref, wproj_ref):
    across = (((1,), (1,)), ((), ()))
    left = iota((512, 128), 1) < HEAD
    zero = jnp.zeros((512, 128), BF)
    ones = jnp.ones((16, 512), BF)
    made = jnp.dot(normed, weights_ref[...], preferred_element_type=F32)
    queries = (made[:, :256] * (HEAD**-0.5 * math.log2(math.e))).astype(BF)
    keys = made[:, 256:512].astype(BF)
    values = made[:, 512:].T.astype(BF)

    def score(head):
        pair = slice(128 * (head // 2), 128 * (head // 2 + 1))
        key = keys[:, pair]
        key = jnp.where(left, key, zero) if head % 2 == 0 else jnp.where(left, zero, key)
        return lax.dot_general(key, queries[:, pair], across, preferred_element_type=F32)

    def mix(head, scores):
        top = jnp.max(scores, axis=0, keepdims=True)
        weights = jnp.exp2(scores - top).astype(BF)
        stacked = jnp.concatenate([values[HEAD * head : HEAD * (head + 1)], ones], axis=0)
        mixed = jnp.dot(stacked, weights, preferred_element_type=F32)
        return mixed[:HEAD] * (1.0 / mixed[HEAD : HEAD + 1])

    scored = [score(head) for head in range(AHEAD)]
    parts = []
    for head in range(4):
        if head + AHEAD < 4:
            scored.append(score(head + AHEAD))
        parts.append(mix(head, scored[head]))
    attended = jnp.concatenate(parts, axis=0).T.astype(BF)
    return jnp.dot(attended, wproj_ref[...], preferred_element_type=F32)


def first_kernel(
    where_ref, recv_hbm, seat_hbm, base_hbm, mine_hbm, swap_hbm, wproj_hbm, gain_ref, bias_ref, pbias_ref,
    total_ref, normed_ref, recv_ref, seat_ref, base_ref, weights_ref, wproj_ref, rows_ref, sems,
):
    clip = pl.program_id(0)
    moves = [
        pltpu.make_async_copy(source, into, sems.at[14 + n])
        for n, (source, into) in enumerate(
            (
                (recv_hbm, recv_ref), (seat_hbm, seat_ref),
                (base_hbm.at[0], base_ref.at[0]), (base_hbm.at[1], base_ref.at[1]),
            )
        )
    ]
    blocks = fetch_blocks(where_ref, 4, mine_hbm, swap_hbm, wproj_hbm, weights_ref, wproj_ref, sems)

    @pl.when(clip == 0)
    def _():
        for move in moves + blocks:
            move.start()
        moves[0].wait()
        rows_ref[...] = recv_ref[...].astype(F32)
        moves[1].wait()
        moves[2].wait()

    @pl.when(clip == 1)
    def _():
        moves[3].wait()

    tokens = jnp.concatenate(
        [rows_ref[pl.ds(4 * clip + part, VMAX, stride=8), :] for part in range(4)], axis=1
    ).astype(BF)
    total_ref[0, :VMAX, :] = jnp.dot(seat_ref[clip], tokens, preferred_element_type=F32)
    for low in range(0, 512, CHUNK):
        rows = slice(low, low + CHUNK)
        values = base_ref[clip, rows, :]
        if low < VMAX:
            values = values + total_ref[0, rows, :]
        average = jnp.mean(values, axis=1, keepdims=True)
        centred = values - average
        spread = jnp.mean(centred * centred, axis=1, keepdims=True)
        normed_ref[0, rows, :] = (
            centred * lax.rsqrt(spread + EPS) * gain_ref[...] + bias_ref[...]
        ).astype(BF)
        total_ref[0, rows, :] = values + pbias_ref[...]

    @pl.when(clip == 0)
    def _():
        for move in blocks:
            move.wait()

    total_ref[0] += four_heads(normed_ref[0], weights_ref, wproj_ref)


def second_kernel(
    where_ref, total_ref, normed_ref, mine_hbm, swap_hbm, wproj_hbm, out_ref, weights_ref, wproj_ref, sems
):
    @pl.when(pl.program_id(0) == 0)
    def _():
        moves = fetch_blocks(where_ref, 6, mine_hbm, swap_hbm, wproj_hbm, weights_ref, wproj_ref, sems)
        for move in moves:
            move.start()
        for move in moves:
            move.wait()

    share = four_heads(normed_ref[0], weights_ref, wproj_ref)
    out_ref[0] = (total_ref[0] + share).astype(BF)


def gather_table():
    table = np.zeros((12, 8), np.int32)
    for z in range(12):
        table[z, :3] = [(0, 2, 1)[(kind - z // 4) % 3] for kind in range(3)]
        table[z, 4:] = [z % 4, (z ^ 2) % 4, (z ^ 1) % 4, (z ^ 3) % 4]
    return table


def whole(shape):
    return pl.BlockSpec(shape, lambda *_: (0,) * len(shape))


def on_device(
    enc_out, norm_gain, norm_bias, w_e2d, token_index, counts, owner, dec_tubes,
    mask_token, dec_gain, dec_bias, w_qkv, w_proj, proj_bias,
):
    vmem = pl.BlockSpec(memory_space=pltpu.VMEM)
    smem = pl.BlockSpec(memory_space=pltpu.SMEM)
    hbm = pl.BlockSpec(memory_space=pltpu.HBM)
    my_index = lax.axis_index(DP).astype(jnp.int32)
    core = lax.axis_index("core").astype(jnp.int32)

    shards = pl.pallas_call(
        shard_kernel,
        out_shape=jax.ShapeDtypeStruct((32, 24, 512), BF),
        in_specs=[smem, vmem],
        compiler_params=pltpu.CompilerParams(vmem_limit_bytes=8 * MIB),
        name="shards",
    )(token_index, w_e2d)
    gathered = lax.all_to_all(shards, PLANE, 0, 0, tiled=True)
    own = gathered.reshape(768, 512)
    other = lax.ppermute(own, "core", [(0, 1), (1, 0)])

    half = lax.dynamic_slice(w_qkv, (core * 256, 0), (256, 128))[None]
    above = lax.ppermute(half, "fsdp", [(z, (z + 4) % 12) for z in range(12)])
    below = lax.ppermute(half, "fsdp", [(z, (z + 8) % 12) for z in range(12)])

    ids = jnp.stack([my_index, core])
    normed, pick, info = pl.pallas_call(
        prep_kernel,
        out_shape=(
            jax.ShapeDtypeStruct((2, VMAX, 768), BF),
            jax.ShapeDtypeStruct((640, VMAX), BF),
            jax.ShapeDtypeStruct((8, 128), jnp.int32),
        ),
        in_specs=[smem] * 2 + [vmem] * 5,
        compiler_params=pltpu.CompilerParams(vmem_limit_bytes=24 * MIB),
        cost_estimate=pl.CostEstimate(flops=4_000_000_000, bytes_accessed=4_000_000, transcendentals=0),
        name="prep",
    )(ids, token_index, enc_out[0], norm_gain[None], norm_bias[None], counts, owner)

    sent = pl.pallas_call(
        embed_kernel,
        out_shape=jax.ShapeDtypeStruct((2560, 128), BF),
        scratch_shapes=[pltpu.VMEM((2560, 128), F32)],
        compiler_params=pltpu.CompilerParams(vmem_limit_bytes=24 * MIB),
        cost_estimate=pl.CostEstimate(flops=1_000_000_000, bytes_accessed=4_000_000, transcendentals=0),
        name="embed",
    )(normed, own, other, pick)

    above, below = lax.optimization_barrier((above, below, sent))[:2]
    three = jnp.concatenate([half, above, below])
    twin = lax.ppermute(three, "fsdp", [(z, z ^ 2) for z in range(12)])
    received = lax.all_to_all(sent.reshape(NDEV, 40, 128), DP, 0, 0, tiled=True)
    received = received.reshape(2560, 128)
    six = jnp.concatenate([three, twin])
    rest = lax.ppermute(six, "fsdp", [(z, z ^ 1) for z in range(12)])
    six_swap = lax.ppermute(six, "core", [(0, 1), (1, 0)])
    rest_swap = lax.ppermute(rest, "core", [(0, 1), (1, 0)])
    where = jnp.asarray(gather_table())[lax.axis_index("fsdp")]
    where = where + core * jnp.asarray(np.arange(8) == 3, np.int32)

    own_mark = own.reshape(32, 24, 512)[:, 22, 0]
    other_mark = other.reshape(32, 24, 512)[:, 22, 0]
    first_mark = jnp.where(core == 0, own_mark, other_mark)
    second_mark = jnp.where(core == 0, other_mark, own_mark)
    marks = jnp.stack([first_mark, second_mark], axis=1).reshape(NDEV).astype(jnp.int32)
    offered = (marks[:, None] * 8 + jnp.arange(PER, dtype=jnp.int32)).reshape(NDEV * PER)
    base, seat = pl.pallas_call(
        codes_kernel,
        out_shape=(pltpu.HBM((2, 512, 512), F32), pltpu.HBM((2, VMAX, VMAX), BF)),
        in_specs=[vmem] * 5,
        compiler_params=pltpu.CompilerParams(vmem_limit_bytes=CODES * MIB),
        cost_estimate=pl.CostEstimate(flops=500_000_000, bytes_accessed=3_000_000, transcendentals=0),
        name="codes",
    )(dec_tubes[0], jnp.asarray(turn_table()), mask_token[None], info, offered[None])

    clip_block = pl.BlockSpec((1, 512, 512), lambda clip: (clip, 0, 0))
    total, dec_normed = pl.pallas_call(
        first_kernel,
        grid=(2,),
        out_shape=(jax.ShapeDtypeStruct((2, 512, 512), F32), jax.ShapeDtypeStruct((2, 512, 512), BF)),
        in_specs=[smem, pl.BlockSpec(memory_space=pl.ANY)] + [hbm] * 5 + [whole((1, 512))] * 3,
        out_specs=(clip_block, clip_block),
        scratch_shapes=[
            pltpu.VMEM((2560, 128), BF),
            pltpu.VMEM((2, VMAX, VMAX), BF),
            pltpu.VMEM((2, 512, 512), F32),
            pltpu.VMEM((512, 768), BF),
            pltpu.VMEM((256, 512), BF),
            pltpu.VMEM((2560, 128), F32),
            pltpu.SemaphoreType.DMA((18,)),
        ],
        compiler_params=pltpu.CompilerParams(vmem_limit_bytes=FIRST * MIB),
        cost_estimate=pl.CostEstimate(flops=2_000_000_000, bytes_accessed=8_000_000, transcendentals=2_000_000),
        name="heads1",
    )(where, received, seat, base, six, six_swap, w_proj, dec_gain[None], dec_bias[None], proj_bias[None])
    return pl.pallas_call(
        second_kernel,
        grid=(2,),
        out_shape=jax.ShapeDtypeStruct((1, 2, 512, 512), BF),
        in_specs=[smem, clip_block, clip_block, hbm, hbm, hbm],
        out_specs=pl.BlockSpec((None, 1, 512, 512), lambda clip: (0, clip, 0, 0)),
        scratch_shapes=[
            pltpu.VMEM((512, 768), BF),
            pltpu.VMEM((256, 512), BF),
            pltpu.SemaphoreType.DMA((14,)),
        ],
        compiler_params=pltpu.CompilerParams(vmem_limit_bytes=SECOND * MIB),
        cost_estimate=pl.CostEstimate(flops=2_000_000_000, bytes_accessed=8_000_000, transcendentals=2_000_000),
        name="heads2",
    )(where, total, dec_normed, rest, rest_swap, w_proj)


def solution(mesh):
    grid = Mesh(np.asarray(mesh.devices).reshape(8, 4, 2, 12), (*DP, "fsdp"))
    return jax.shard_map(
        on_device,
        mesh=grid,
        in_specs=(
            P("fsdp", DP, None), P(), P(), P(DP, None), P("fsdp", DP), P("fsdp", None), P("fsdp", None),
            P("fsdp", DP, None), P(), P(), P(), P(None, "fsdp"), P(), P(),
        ),
        out_specs=P("fsdp", DP, None, None),
        check_vma=False,
    )
```

```python
import math

import jax
import jax.numpy as jnp
import numpy as np
from jax import lax
from jax.experimental import pallas as pl
from jax.experimental.pallas import tpu as pltpu
from jax.sharding import Mesh, PartitionSpec as P

DP = ("y", "x", "core")
PLANE = ("y", "x")
HEAD = 64
VMAX = 320
NDEV = 64
PER = 5
FIRST = 53
CODES = 16
SECOND = 53
AHEAD = 2
CHUNK = 64
EPS = 1e-06
MIB = 1 << 20
BF = jnp.bfloat16
F32 = jnp.float32


def iota(shape, dim):
    return lax.broadcasted_iota(jnp.int32, shape, dim)


def prep_kernel(ids_ref, token_ref, enc_ref, gain_ref, bias_ref, counts_ref, owner_ref, normed_ref, pick_ref, info_ref):
    residue = token_ref[0, 0] & 63
    my_index = ids_ref[0]
    core = ids_ref[1]
    counts = counts_ref[...].astype(F32)
    row_id = iota((128, 128), 0)
    col_id = iota((128, 128), 1)
    counts_col = jnp.sum(jnp.where(row_id == col_id, counts, 0.0), axis=1, keepdims=True)
    first = jnp.sum(jnp.where(row_id < col_id, counts_col, 0.0), axis=0, keepdims=True)
    owner = owner_ref[...]
    start = jnp.floor((first + (63 - residue).astype(F32)) * (1.0 / 64.0))
    place = iota((640, 128), 0)
    dest = (place * 6554) >> 16
    rest = place - 10 * dest
    slot = 2 * dest + (rest & 1)
    target = jnp.sum(jnp.where(owner == slot, start, 0.0), axis=1, keepdims=True)
    target = target.astype(jnp.int32) + (rest >> 1)[:, :1]
    pick_ref[...] = jnp.where(iota((640, VMAX), 1) == target, 1.0, 0.0).astype(BF)
    line = iota((8, 128), 0)
    mine = 2 * my_index + (line & 1)
    held = jnp.where(line < 2, first, counts)
    info = jnp.sum(jnp.where(owner == mine, held, 0.0), axis=1, keepdims=True)
    info_ref[...] = jnp.broadcast_to(info, (8, 128)).astype(jnp.int32)
    values = enc_ref[...].astype(F32)
    average = jnp.mean(values, axis=1, keepdims=True)
    centred = values - average
    spread = jnp.mean(centred * centred, axis=1, keepdims=True)
    normed = (centred * lax.rsqrt(spread + EPS) * gain_ref[...] + bias_ref[...]).astype(BF)
    for half in range(2):
        side = core if half == 0 else 1 - core
        for tile, (low, high) in enumerate(((0, 512), (384, 1024), (896, 1408))):
            size = high - low
            column = iota((1, 256), 1) + 256 * tile
            block = (column * 2731) >> 16
            inner = column - 24 * block
            source = jnp.where(inner < 22, 44 * block + 22 * side + inner - low, -1)
            spread_out = jnp.where(iota((size, 256), 0) == source, 1.0, 0.0).astype(BF)
            normed_ref[half, :, 256 * tile : 256 * (tile + 1)] = jnp.dot(
                normed[:, low:high], spread_out, preferred_element_type=F32
            ).astype(BF)


def embed_kernel(normed_ref, own_ref, other_ref, pick_ref, out_ref, rows_ref):
    embedded = jnp.dot(normed_ref[0], own_ref[...], preferred_element_type=F32)
    embedded += jnp.dot(normed_ref[1], other_ref[...], preferred_element_type=F32)
    embedded = embedded.astype(BF)
    packed = jnp.dot(pick_ref[...], embedded, preferred_element_type=F32)
    for part in range(4):
        rows_ref[pl.ds(part, 640, stride=4), :] = packed[:, 128 * part : 128 * (part + 1)]
    out_ref[...] = rows_ref[:2560, :].astype(BF)


def shard_kernel(ids_ref, rows_ref, out_ref):
    residue = (ids_ref[0, 0] & 63).astype(F32)
    mark = jnp.full((2, 512), residue, F32)
    block = jnp.concatenate([rows_ref[...].astype(F32), mark], axis=0).astype(BF)
    for chip in range(32):
        out_ref[chip] = block


def turn_table():
    column = np.arange(512)
    turns = np.power(10000.0, -(2 * (column // 2)) / 512.0) / (2 * math.pi)
    scale = np.exp2(np.floor(np.log2(turns)) - 10)
    high = np.floor(turns / scale) * scale
    return np.stack([high, turns - high, 0.25 * (column % 2)]).astype(np.float32)


def codes_kernel(tubes_ref, table_ref, mask_ref, info_ref, offered_ref, base_ref, seat_ref):
    info = info_ref[...]
    for clip in range(2):
        tubes = jnp.broadcast_to(tubes_ref[clip : clip + 1, :].astype(F32), (8, 512)).T[:, :1]
        count = info[2 + clip : 3 + clip, :1]
        for low in range(0, 512, 64):
            tube = tubes[low : low + 64]
            whole_turns = tube * table_ref[0:1, :]
            turn = whole_turns - jnp.round(whole_turns) + (tube * table_ref[1:2, :] + table_ref[2:3, :])
            turn = turn - jnp.round(turn)
            size = jnp.abs(turn)
            angle = jnp.minimum(size, 0.5 - size) * (2 * math.pi)
            square = angle * angle
            series = 1.0 / 362880 - square * (1.0 / 39916800)
            for power in (5040, 120, 6, 1):
                series = 1.0 / power - square * series
            sine = angle * series
            code = jnp.where(turn < 0, -sine, sine)
            hidden = iota((64, 512), 0) + low >= count
            base_ref[clip, low : low + 64, :] = jnp.where(hidden, mask_ref[...], 0.0) + code
        rank = iota((VMAX, 1), 0)
        wanted = ((info[clip : clip + 1, :1] + rank) & 63) * 8 + (rank >> 6)
        wanted = jnp.where(rank < count, wanted, -1)
        seat_ref[clip] = jnp.where(offered_ref[...] == wanted, 1.0, 0.0).astype(BF)


def fetch_blocks(where_ref, first, mine_hbm, swap_hbm, wproj_hbm, weights_ref, wproj_ref, sems):
    moves = []

    def move(source, into):
        moves.append(pltpu.make_async_copy(source, into, sems.at[len(moves)]))

    for pair in range(2):
        for kind in range(3):
            at = 3 * pair + where_ref[kind]
            column = 256 * kind + 128 * pair
            for source, side in ((mine_hbm, where_ref[3]), (swap_hbm, 1 - where_ref[3])):
                rows = pl.ds(pl.multiple_of(256 * side, 256), 256)
                move(source.at[at], weights_ref.at[rows, column : column + 128])
        rows = pl.ds(pl.multiple_of(128 * where_ref[first + pair], 128), 128)
        move(wproj_hbm.at[rows, :], wproj_ref.at[128 * pair : 128 * (pair + 1), :])
    return moves


def four_heads(normed, weights_ref, wproj_ref):
    across = (((1,), (1,)), ((), ()))
    left = iota((512, 128), 1) < HEAD
    zero = jnp.zeros((512, 128), BF)
    ones = jnp.ones((16, 512), BF)
    made = jnp.dot(normed, weights_ref[...], preferred_element_type=F32)
    queries = (made[:, :256] * (HEAD**-0.5 * math.log2(math.e))).astype(BF)
    keys = made[:, 256:512].astype(BF)
    values = made[:, 512:].T.astype(BF)

    def score(head):
        pair = slice(128 * (head // 2), 128 * (head // 2 + 1))
        key = keys[:, pair]
        key = jnp.where(left, key, zero) if head % 2 == 0 else jnp.where(left, zero, key)
        return lax.dot_general(key, queries[:, pair], across, preferred_element_type=F32)

    def mix(head, scores):
        top = jnp.max(scores, axis=0, keepdims=True)
        weights = jnp.exp2(scores - top).astype(BF)
        stacked = jnp.concatenate([values[HEAD * head : HEAD * (head + 1)], ones], axis=0)
        mixed = jnp.dot(stacked, weights, preferred_element_type=F32)
        return mixed[:HEAD] * (1.0 / mixed[HEAD : HEAD + 1])

    scored = [score(head) for head in range(AHEAD)]
    parts = []
    for head in range(4):
        if head + AHEAD < 4:
            scored.append(score(head + AHEAD))
        parts.append(mix(head, scored[head]))
    attended = jnp.concatenate(parts, axis=0).T.astype(BF)
    return jnp.dot(attended, wproj_ref[...], preferred_element_type=F32)


def first_kernel(
    where_ref, recv_hbm, seat_hbm, base_hbm, mine_hbm, swap_hbm, wproj_hbm, gain_ref, bias_ref, pbias_ref,
    total_ref, normed_ref, recv_ref, seat_ref, base_ref, weights_ref, wproj_ref, rows_ref, sems,
):
    clip = pl.program_id(0)
    moves = [
        pltpu.make_async_copy(source, into, sems.at[14 + n])
        for n, (source, into) in enumerate(
            (
                (recv_hbm, recv_ref), (seat_hbm, seat_ref),
                (base_hbm.at[0], base_ref.at[0]), (base_hbm.at[1], base_ref.at[1]),
            )
        )
    ]
    blocks = fetch_blocks(where_ref, 4, mine_hbm, swap_hbm, wproj_hbm, weights_ref, wproj_ref, sems)

    @pl.when(clip == 0)
    def _():
        for move in moves + blocks:
            move.start()
        moves[0].wait()
        rows_ref[:2560, :] = recv_ref[...].astype(F32)
        moves[1].wait()
        moves[2].wait()

    @pl.when(clip == 1)
    def _():
        moves[3].wait()

    tokens = jnp.concatenate(
        [rows_ref[pl.ds(4 * clip + part, VMAX, stride=8), :] for part in range(4)], axis=1
    ).astype(BF)
    total_ref[0, :VMAX, :] = jnp.dot(seat_ref[clip], tokens, preferred_element_type=F32)
    for low in range(0, 512, CHUNK):
        rows = slice(low, low + CHUNK)
        values = base_ref[clip, rows, :]
        if low < VMAX:
            values = values + total_ref[0, rows, :]
        average = jnp.mean(values, axis=1, keepdims=True)
        centred = values - average
        spread = jnp.mean(centred * centred, axis=1, keepdims=True)
        normed_ref[0, rows, :] = (
            centred * lax.rsqrt(spread + EPS) * gain_ref[...] + bias_ref[...]
        ).astype(BF)
        total_ref[0, rows, :] = values + pbias_ref[...]

    @pl.when(clip == 0)
    def _():
        for move in blocks:
            move.wait()

    total_ref[0] += four_heads(normed_ref[0], weights_ref, wproj_ref)


def second_kernel(
    where_ref, total_ref, normed_ref, mine_hbm, swap_hbm, wproj_hbm, out_ref, weights_ref, wproj_ref, sems
):
    @pl.when(pl.program_id(0) == 0)
    def _():
        moves = fetch_blocks(where_ref, 6, mine_hbm, swap_hbm, wproj_hbm, weights_ref, wproj_ref, sems)
        for move in moves:
            move.start()
        for move in moves:
            move.wait()

    share = four_heads(normed_ref[0], weights_ref, wproj_ref)
    out_ref[0] = (total_ref[0] + share).astype(BF)


def gather_table():
    table = np.zeros((12, 8), np.int32)
    for z in range(12):
        table[z, :3] = [(0, 2, 1)[(kind - z // 4) % 3] for kind in range(3)]
        table[z, 4:] = [z % 4, (z ^ 2) % 4, (z ^ 1) % 4, (z ^ 3) % 4]
    return table


def whole(shape):
    return pl.BlockSpec(shape, lambda *_: (0,) * len(shape))


def on_device(
    enc_out, norm_gain, norm_bias, w_e2d, token_index, counts, owner, dec_tubes,
    mask_token, dec_gain, dec_bias, w_qkv, w_proj, proj_bias,
):
    vmem = pl.BlockSpec(memory_space=pltpu.VMEM)
    smem = pl.BlockSpec(memory_space=pltpu.SMEM)
    hbm = pl.BlockSpec(memory_space=pltpu.HBM)
    my_index = lax.axis_index(DP).astype(jnp.int32)
    core = lax.axis_index("core").astype(jnp.int32)

    shards = pl.pallas_call(
        shard_kernel,
        out_shape=jax.ShapeDtypeStruct((32, 24, 512), BF),
        in_specs=[smem, vmem],
        compiler_params=pltpu.CompilerParams(vmem_limit_bytes=8 * MIB),
        name="shards",
    )(token_index, w_e2d)
    gathered = lax.all_to_all(shards, PLANE, 0, 0, tiled=True)
    own = gathered.reshape(768, 512)
    other = lax.ppermute(own, "core", [(0, 1), (1, 0)])

    half = lax.dynamic_slice(w_qkv, (core * 256, 0), (256, 128))[None]
    above = lax.ppermute(half, "fsdp", [(z, (z + 4) % 12) for z in range(12)])
    below = lax.ppermute(half, "fsdp", [(z, (z + 8) % 12) for z in range(12)])

    ids = jnp.stack([my_index, core])
    normed, pick, info = pl.pallas_call(
        prep_kernel,
        out_shape=(
            jax.ShapeDtypeStruct((2, VMAX, 768), BF),
            jax.ShapeDtypeStruct((640, VMAX), BF),
            jax.ShapeDtypeStruct((8, 128), jnp.int32),
        ),
        in_specs=[smem] * 2 + [vmem] * 5,
        compiler_params=pltpu.CompilerParams(vmem_limit_bytes=24 * MIB),
        cost_estimate=pl.CostEstimate(flops=4_000_000_000, bytes_accessed=4_000_000, transcendentals=0),
        name="prep",
    )(ids, token_index, enc_out[0], norm_gain[None], norm_bias[None], counts, owner)

    sent = pl.pallas_call(
        embed_kernel,
        out_shape=jax.ShapeDtypeStruct((2560, 128), BF),
        scratch_shapes=[pltpu.VMEM((2624, 128), F32)],
        compiler_params=pltpu.CompilerParams(vmem_limit_bytes=24 * MIB),
        cost_estimate=pl.CostEstimate(flops=1_000_000_000, bytes_accessed=4_000_000, transcendentals=0),
        name="embed",
    )(normed, own, other, pick)

    above, below = lax.optimization_barrier((above, below, sent))[:2]
    three = jnp.concatenate([half, above, below])
    twin = lax.ppermute(three, "fsdp", [(z, z ^ 2) for z in range(12)])
    received = lax.all_to_all(sent.reshape(NDEV, 40, 128), DP, 0, 0, tiled=True)
    received = received.reshape(2560, 128)
    six = jnp.concatenate([three, twin])
    rest = lax.ppermute(six, "fsdp", [(z, z ^ 1) for z in range(12)])
    six_swap = lax.ppermute(six, "core", [(0, 1), (1, 0)])
    rest_swap = lax.ppermute(rest, "core", [(0, 1), (1, 0)])
    where = jnp.asarray(gather_table())[lax.axis_index("fsdp")]
    where = where + core * jnp.asarray(np.arange(8) == 3, np.int32)

    own_mark = own.reshape(32, 24, 512)[:, 22, 0]
    other_mark = other.reshape(32, 24, 512)[:, 22, 0]
    first_mark = jnp.where(core == 0, own_mark, other_mark)
    second_mark = jnp.where(core == 0, other_mark, own_mark)
    marks = jnp.stack([first_mark, second_mark], axis=1).reshape(NDEV).astype(jnp.int32)
    offered = (marks[:, None] * 8 + jnp.arange(PER, dtype=jnp.int32)).reshape(NDEV * PER)
    base, seat = pl.pallas_call(
        codes_kernel,
        out_shape=(pltpu.HBM((2, 512, 512), F32), pltpu.HBM((2, VMAX, VMAX), BF)),
        in_specs=[vmem] * 5,
        compiler_params=pltpu.CompilerParams(vmem_limit_bytes=CODES * MIB),
        cost_estimate=pl.CostEstimate(flops=500_000_000, bytes_accessed=3_000_000, transcendentals=0),
        name="codes",
    )(dec_tubes[0], jnp.asarray(turn_table()), mask_token[None], info, offered[None])

    clip_block = pl.BlockSpec((1, 512, 512), lambda clip: (clip, 0, 0))
    total, dec_normed = pl.pallas_call(
        first_kernel,
        grid=(2,),
        out_shape=(jax.ShapeDtypeStruct((2, 512, 512), F32), jax.ShapeDtypeStruct((2, 512, 512), BF)),
        in_specs=[smem, pl.BlockSpec(memory_space=pl.ANY)] + [hbm] * 5 + [whole((1, 512))] * 3,
        out_specs=(clip_block, clip_block),
        scratch_shapes=[
            pltpu.VMEM((2560, 128), BF),
            pltpu.VMEM((2, VMAX, VMAX), BF),
            pltpu.VMEM((2, 512, 512), F32),
            pltpu.VMEM((512, 768), BF),
            pltpu.VMEM((256, 512), BF),
            pltpu.VMEM((2624, 128), F32),
            pltpu.SemaphoreType.DMA((18,)),
        ],
        compiler_params=pltpu.CompilerParams(vmem_limit_bytes=FIRST * MIB),
        cost_estimate=pl.CostEstimate(flops=2_000_000_000, bytes_accessed=8_000_000, transcendentals=2_000_000),
        name="heads1",
    )(where, received, seat, base, six, six_swap, w_proj, dec_gain[None], dec_bias[None], proj_bias[None])
    return pl.pallas_call(
        second_kernel,
        grid=(2,),
        out_shape=jax.ShapeDtypeStruct((1, 2, 512, 512), BF),
        in_specs=[smem, clip_block, clip_block, hbm, hbm, hbm],
        out_specs=pl.BlockSpec((None, 1, 512, 512), lambda clip: (0, clip, 0, 0)),
        scratch_shapes=[
            pltpu.VMEM((512, 768), BF),
            pltpu.VMEM((256, 512), BF),
            pltpu.SemaphoreType.DMA((14,)),
        ],
        compiler_params=pltpu.CompilerParams(vmem_limit_bytes=SECOND * MIB),
        cost_estimate=pl.CostEstimate(flops=2_000_000_000, bytes_accessed=8_000_000, transcendentals=2_000_000),
        name="heads2",
    )(where, total, dec_normed, rest, rest_swap, w_proj)


def solution(mesh):
    grid = Mesh(np.asarray(mesh.devices).reshape(8, 4, 2, 12), (*DP, "fsdp"))
    return jax.shard_map(
        on_device,
        mesh=grid,
        in_specs=(
            P("fsdp", DP, None), P(), P(), P(DP, None), P("fsdp", DP), P("fsdp", None), P("fsdp", None),
            P("fsdp", DP, None), P(), P(), P(), P(None, "fsdp"), P(), P(),
        ),
        out_specs=P("fsdp", DP, None, None),
        check_vma=False,
    )
```
